128 devices in a mesh: dp: 2 (over x_lo), expert: 64 (over y, z, x_hi, core).
Axes of the slice: x: 4 (x_hi: 2, x_lo: 2; x = x_hi * 2 + x_lo), y: 4, z: 4, core: 2. Of those that a mesh axis runs over, the one named last changes fastest.
Arguments:
- tokens: bfloat16 [16384, 2048], P(('dp', 'expert')), may hold values from -6 to 6
- cotangent: bfloat16 [16384, 2048], P(('dp', 'expert')), may hold values from -6 to 6
- expert_ids: int32 [16384, 4], P(('dp', 'expert')), may hold values from 0 to 63, all different within a row; in each aligned block of 128 rows (0 to 127, 128 to 255, ...) at most 12 rows name the same one
- combine: float32 [16384, 4], P(('dp', 'expert')), may hold values from 0.1 to 1
- placement: int32 [64], replicated, may hold values from 0 to 63, each once
- moves: int32 [64], replicated, may hold values from 0 to 1, as said below
- w_gate: bfloat16 [64, 2048, 768], P('expert'), may hold values from -0.125 to 0.125
- w_up: bfloat16 [64, 2048, 768], P('expert'), may hold values from -0.125 to 0.125
- w_down: bfloat16 [64, 768, 2048], P('expert'), may hold values from -0.21875 to 0.21875
Outputs:
- mixed: bfloat16 [16384, 2048], P(('dp', 'expert'))
- input_grad: bfloat16 [16384, 2048], P(('dp', 'expert'))
- grad_gate: float32 [64, 2048, 768], P('expert', 'dp')
- grad_up: float32 [64, 2048, 768], P('expert', 'dp')
- grad_down: float32 [64, 768, 2048], P('expert', 'dp')
The draws below stay inside these ranges and needn't reach their ends.
Inputs may be any that keep to these rules, and one draw needn't show every extreme that they name: `expert_ids`: each row names 4 different experts. In the rows of one device no expert is named more than 12 times, a bound that some block reaches. `placement`: A permutation of the experts. moves[d] = moves[(d + 32) mod 64]; at least one pair exchanges and at least one does not.
All inputs are finite; a program needn't handle non-finite values.
Results may differ from the reference program's by a relative error of at most 0.0064.
Values may be sent and summed in bfloat16 or wider, within the bound.
A program may use at most 192 MiB of HBM per device.

```python
import math
import jax
import jax.numpy as jnp
import numpy as np
from jax import lax

D = 2048
FF = 768
TOPK = 4
TOK_DEV = 128
EXPERTS = 64
CAP = 12
TOKENS = 16384
N_DP = 2


def draw_moves(key, part):
    half_count = EXPERTS // 2
    pair_bits = jax.random.randint(jax.random.fold_in(key, 11), (half_count,), 0, 2).astype(jnp.int32)
    pair_bits = pair_bits.at[0].set(1).at[1].set(0).at[half_count - 1].set(1)
    return jnp.concatenate([pair_bits, pair_bits]).astype(jnp.int32)


def block_levels(stream_key, shape, split, least, high):
    level = 1.0
    for dim, shards_of in split:
        draws = jax.random.uniform(jax.random.fold_in(jax.random.fold_in(stream_key, 6), dim), (shards_of,), jnp.float32, least / len(split), high / len(split))
        level = level * jnp.repeat(jnp.exp(draws), shape[dim] // shards_of).reshape((-1,) + (1,) * (len(shape) - 1 - dim))
    return level


def deal_out(key, own, number, rows, count, top, limit, skew):
    ranking = jax.random.permutation(key, count)
    crowded, ordinary = load_shares(count, rows * top, limit, skew, True), load_shares(count, rows * top, limit, skew, False)
    places = jnp.arange(count)

    def named(lengths, turn):
        used = int((lengths > 0).sum())
        fixed = max(1, used // 4)
        passed = fixed + (places - fixed + turn * (used - fixed)) % max(1, count - fixed)
        return jnp.zeros((count,), jnp.int32).at[ranking[jnp.where(places < fixed, places, passed)]].set(jnp.asarray(lengths, jnp.int32))

    lengths = jnp.where(number % 4 == 0, named(crowded, number // 4), named(ordinary, number - number // 4 - 1))
    mixed = jax.random.permutation(jax.random.fold_in(own, 3), count)
    giver, taker = mixed[0:count // 2 * 2:2], mixed[1:count // 2 * 2:2]
    room = jnp.minimum(lengths[giver] - 1, limit - lengths[taker]) // 2
    room = jnp.where((giver == ranking[0]) | (taker == ranking[0]) | (lengths[taker] == 0), 0, jnp.maximum(room, 0))
    passed = jax.random.randint(jax.random.fold_in(own, 4), (count // 2,), 0, 1 << 20) % (room + 1)
    lengths = lengths.at[giver].add(-passed).at[taker].add(passed)
    items = jnp.searchsorted(jnp.cumsum(lengths), jnp.arange(rows * top), side="right").astype(jnp.int32)
    listing = items.reshape(top, rows).T
    listing = listing[jax.random.permutation(jax.random.fold_in(own, 1), rows)]
    turn = jax.random.randint(jax.random.fold_in(own, 2), (rows, 1), 0, top)
    return jnp.take_along_axis(listing, (jnp.arange(top)[None, :] + turn) % top, axis=1)


def load_shares(count, total, most, slope, full):
    loads = [(1 << 20) // math.isqrt(grade ** slope) + 1 for grade in range(1, count + 1)]
    largest = most if full else min(most, max(-(-total // count), total * loads[0] // sum(loads)))
    least = 1 if total - largest >= count - 1 else 0
    holding, surplus = [largest] + [least] * (count - 1), total - largest - least * (count - 1)
    while surplus > 0:
        movable = [i for i in range(1, count) if holding[i] < largest] or [i for i in range(1, count) if holding[i] < most]
        mass, left = sum([loads[i] for i in movable]), surplus
        for i in movable:
            more = min(most - holding[i], max(1, left * loads[i] // mass), surplus)
            holding[i] = holding[i] + more
            surplus = surplus - more
    return np.array(holding)


def noise(rng, extent, deviation, limit, pieces=(), held_as=jnp.bfloat16):
    result = jax.random.normal(rng, extent, jnp.float32) * deviation
    if len(pieces) > 0:
        result = block_levels(rng, extent, pieces, -0.22, 0.18) * result
    return jnp.clip(result, min=-limit, max=limit).astype(held_as)


def setup_inputs(seed: int = 0) -> dict:
    splits = jax.random.split(jax.random.key(seed), 10)
    tokens = noise(splits[0], (TOKENS, D), 1.0, 6.0, ((0, 128),))
    cotangent = noise(splits[1], (TOKENS, D), 1.0, 6.0, ((0, 128),))
    expert_ids_keys = jax.random.split(jax.random.fold_in(splits[2], 1), TOKENS // TOK_DEV)
    expert_ids_turns = jax.random.permutation(jax.random.fold_in(splits[2], 3), TOKENS // TOK_DEV)
    expert_ids = jax.vmap(lambda own, number: deal_out(jax.random.fold_in(splits[2], 2), own, number, TOK_DEV, EXPERTS, TOPK, CAP, 2))(expert_ids_keys, expert_ids_turns).reshape((TOKENS, TOPK))
    combine = jnp.clip(jnp.exp(math.log(1.0) - 2.3025851 * jax.random.uniform(splits[3], (TOKENS, TOPK), jnp.float32) ** block_levels(splits[3], (TOKENS, TOPK), ((0, 128),), -0.2, 0.2)), 0.1, 1.0)
    placement = jax.random.permutation(splits[4], EXPERTS).astype(jnp.int32)
    moves = draw_moves(jax.random.fold_in(splits[9], 71), 0)
    w_gate = noise(splits[6], (EXPERTS, D, FF), D ** -0.5, 0.125, ((0, 64),))
    w_up = noise(splits[7], (EXPERTS, D, FF), D ** -0.5, 0.125, ((0, 64),))
    w_down = noise(splits[8], (EXPERTS, FF, D), FF ** -0.5, 0.21875, ((0, 64),))
    return {"tokens": tokens, "cotangent": cotangent, "expert_ids": expert_ids, "combine": combine, "placement": placement, "moves": moves, "w_gate": w_gate, "w_up": w_up, "w_down": w_down}


def reference(tokens, cotangent, expert_ids, combine, placement, moves, w_gate, w_up, w_down):
    slot_ids = jnp.arange(EXPERTS, dtype=jnp.int32)
    held_expert = jnp.where(moves == 1, jnp.roll(placement, EXPERTS // 2), placement)
    home_slots = jnp.zeros((EXPERTS,), jnp.int32).at[placement].set(slot_ids)
    flat_ids = expert_ids.reshape(-1)
    flat_weights = combine.reshape(-1)
    token_of = (jnp.arange(TOKENS * TOPK, dtype=jnp.int32) // TOPK).astype(jnp.int32)
    max_rows = CAP * (TOKENS // TOK_DEV)
    contract_rows = (((0,), (0,)), ((), ()))
    contract_last = (((1,), (1,)), ((), ()))

    def per_expert(carry, expert):
        mixed_acc, grad_acc = carry
        chosen = flat_ids == expert
        hits = jnp.nonzero(chosen, size=max_rows, fill_value=0)[0].astype(jnp.int32)
        live_rows = (jnp.arange(max_rows, dtype=jnp.int32) < jnp.sum(chosen.astype(jnp.int32))).astype(jnp.float32)
        row_index = token_of[hits]
        row_inputs = tokens[row_index]
        row_weights = flat_weights[hits] * live_rows
        out_grad = (row_weights[:, None] * cotangent[row_index].astype(jnp.float32)).astype(jnp.bfloat16)
        home_slot = home_slots[expert]
        gate_weight = w_gate[home_slot]
        up_weight = w_up[home_slot]
        down_weight = w_down[home_slot]
        gate_pre = jnp.dot(row_inputs, gate_weight, preferred_element_type=jnp.float32)
        up_pre = jnp.dot(row_inputs, up_weight, preferred_element_type=jnp.float32)
        sigma = jax.nn.sigmoid(gate_pre)
        hidden = (gate_pre * sigma * up_pre).astype(jnp.bfloat16)
        expert_out = jnp.dot(hidden, down_weight, preferred_element_type=jnp.float32).astype(jnp.bfloat16)
        mixed_acc = mixed_acc.at[row_index].add(row_weights[:, None] * expert_out.astype(jnp.float32))
        hidden_grad = lax.dot_general(out_grad, down_weight, contract_last, preferred_element_type=jnp.float32)
        gate_grad = (hidden_grad * up_pre * sigma * (1.0 + gate_pre * (1.0 - sigma))).astype(jnp.bfloat16)
        up_grad = (hidden_grad * gate_pre * sigma).astype(jnp.bfloat16)
        row_grad = (lax.dot_general(gate_grad, gate_weight, contract_last, preferred_element_type=jnp.float32)
                    + lax.dot_general(up_grad, up_weight, contract_last, preferred_element_type=jnp.float32)).astype(jnp.bfloat16)
        grad_acc = grad_acc.at[row_index].add(live_rows[:, None] * row_grad.astype(jnp.float32))
        g_gate = lax.dot_general(row_inputs, gate_grad, contract_rows, preferred_element_type=jnp.float32)
        g_up = lax.dot_general(row_inputs, up_grad, contract_rows, preferred_element_type=jnp.float32)
        g_down = lax.dot_general(hidden, out_grad, contract_rows, preferred_element_type=jnp.float32)
        return (mixed_acc, grad_acc), (g_gate, g_up, g_down)

    start = (jnp.zeros((TOKENS, D), jnp.float32), jnp.zeros((TOKENS, D), jnp.float32))
    (mixed_acc, grad_acc), (all_gate, all_up, all_down) = lax.scan(per_expert, start, slot_ids)
    scale = 1.0 / N_DP
    grad_gate = jnp.take(all_gate, held_expert, axis=0) * scale
    grad_up = jnp.take(all_up, held_expert, axis=0) * scale
    grad_down = jnp.take(all_down, held_expert, axis=0) * scale
    return (mixed_acc.astype(jnp.bfloat16), grad_acc.astype(jnp.bfloat16), grad_gate, grad_up, grad_down)
```

```python
import jax
import jax.numpy as jnp
from jax import lax
from jax.experimental import pallas as pl
from jax.experimental.pallas import tpu as pltpu
from jax.sharding import PartitionSpec as P

MESH = pl.DeviceIdType.MESH
BF16 = jnp.bfloat16
F32 = jnp.float32
PLANE = 16
RINGS = 4
CAP = 12
ROWS = RINGS * CAP
TILE = 256
CONTRACT_ROWS = (((0,), (0,)), ((), ()))
CONTRACT_LAST = (((1,), (1,)), ((), ()))


def place():
    p = lax.axis_index("dp")
    e = lax.axis_index("expert")
    return p, lax.rem(e, PLANE), e // PLANE


def plane_peer(p, l, y, r):
    rc, rx, rz = r % 2, (r // 2) % 2, r // 4
    core, xh, z = lax.rem(l, 2), lax.rem(l // 2, 2), l // 4
    j = lax.rem(z + rz, 4) * 4 + lax.rem(xh + rx, 2) * 2 + lax.rem(core + rc, 2)
    return (p if rx == 0 else 1 - p, y * PLANE + j), j


def plane_source(p, l, y, r):
    rc, rx, rz = r % 2, (r // 2) % 2, r // 4
    core, xh, z = lax.rem(l, 2), lax.rem(l // 2, 2), l // 4
    j = lax.rem(z + 4 - rz, 4) * 4 + lax.rem(xh + rx, 2) * 2 + lax.rem(core + rc, 2)
    return (p if rx == 0 else 1 - p, y * PLANE + j), j


def ring_peer(p, l, y, d):
    return (p, lax.rem(y + d, RINGS) * PLANE + l)


def remote(src, dst, send, recv, device):
    return pltpu.make_async_remote_copy(
        src_ref=src, dst_ref=dst, send_sem=send, recv_sem=recv, device_id=device, device_id_type=MESH
    )


def greet(devices):
    barrier = pltpu.get_barrier_semaphore()
    for device in devices:
        pl.semaphore_signal(barrier, inc=1, device_id=device, device_id_type=MESH)
    return lambda: pl.semaphore_wait(barrier, len(devices))


def columns(n):
    return pl.ds(pl.multiple_of(n * TILE, TILE), TILE)


def selection(meta, base, ring):
    m = meta[ring]
    row = (lax.broadcasted_iota(jnp.int32, (PLANE * ROWS, 128), 0) + base).astype(F32)
    hit = jnp.zeros((PLANE * ROWS, 128), F32)
    weight = jnp.zeros((PLANE * ROWS, 128), F32)
    for k in range(4):
        same = row == m[k : k + 1, :]
        hit = jnp.where(same, 1.0, hit)
        weight = jnp.where(same, m[4 + k : 5 + k, :], weight)
    return hit, weight


def dispatch_kernel(
    ids, comb, plc, tok, cot, x_out, og_out, meta, gtok, gcot, pick, rw, sx, so,
    meta_send, meta_recv, ag_send, ag_recv, own_sem, d_send, d_recv,
):
    p, l, y = place()
    width = tok.shape[1]
    half = width // 2
    ring = [ring_peer(p, l, y, d) for d in range(1, RINGS)]
    peers = [plane_peer(p, l, y, r) for r in range(1, PLANE)]
    ready = greet(ring + [d for d, _ in peers])

    slots = plc.shape[0]
    tokens = ids.shape[1]
    slot_id = lax.broadcasted_iota(jnp.int32, (slots, tokens), 0)
    owned = [(plc[...] == ids[k : k + 1, :]) for k in range(4)]
    member = jnp.zeros((slots, tokens), F32)
    for o in owned:
        member = jnp.where(o, 1.0, member)
    before = (
        lax.broadcasted_iota(jnp.int32, (tokens, tokens), 0)
        < lax.broadcasted_iota(jnp.int32, (tokens, tokens), 1)
    ).astype(F32)
    rank = jnp.dot(member.astype(BF16), before.astype(BF16), preferred_element_type=F32)
    position = rank + (slot_id * ROWS + y * CAP).astype(F32)
    rows = [jnp.sum(jnp.where(o, position, 0.0), axis=0, keepdims=True) for o in owned]
    meta[y] = jnp.concatenate(rows + [comb[...]], axis=0)
    own_rows = pl.ds(pl.multiple_of(y * tokens, tokens), tokens)

    ready()
    copies = [
        remote(meta.at[y], meta.at[y], meta_send.at[d], meta_recv.at[d], ring[d]) for d in range(3)
    ]
    gather = []
    for c in range(4):
        src, dst = (tok, gtok) if c < 2 else (cot, gcot)
        cols = pl.ds((c % 2) * half, half)
        gather.append([
            remote(src.at[:, cols], dst.at[own_rows, cols], ag_send.at[c, d], ag_recv.at[c, d], ring[d])
            for d in range(3)
        ])
    for copy in copies + [g for group in gather for g in group]:
        copy.start()
    gtok[own_rows, :] = tok[...]
    gcot[own_rows, :] = cot[...]
    for copy in copies:
        copy.wait_recv()
    for b in range(RINGS):
        hit, weight = selection(meta, y * PLANE * ROWS, b)
        pick[:, b * tokens : (b + 1) * tokens] = hit.astype(BF16)
        total = jnp.sum(weight, axis=1, keepdims=True)
        rw[...] = total if b == 0 else rw[...] + total

    sent, locals_ = [], []
    for c in range(4):
        src, buf, dst = (gtok, sx, x_out) if c < 2 else (gcot, so, og_out)
        cols = pl.ds((c % 2) * half, half)
        for copy in gather[c]:
            copy.wait_recv()

        def step(n, _, src=src, buf=buf, c=c):
            at = columns((c % 2) * (half // TILE) + n)
            got = jnp.dot(pick[...], src[:, at], preferred_element_type=F32)
            if c >= 2:
                got = rw[...] * got
            buf[:, :, at] = got.astype(BF16).reshape(PLANE, ROWS, TILE)
            return 0

        lax.fori_loop(0, half // TILE, step, 0)
        for r, (device, j) in enumerate(peers):
            copy = remote(buf.at[j, :, cols], dst.at[l, :, cols], d_send.at[c, r], d_recv.at[c, r], device)
            copy.start()
            sent.append(copy)
        own = pltpu.make_async_copy(buf.at[l, :, cols], dst.at[l, :, cols], own_sem.at[c])
        own.start()
        locals_.append(own)
    for copy in sent:
        copy.wait()
    for copy in locals_:
        copy.wait()
    for copy in copies + [g for group in gather for g in group]:
        copy.wait_send()


def dispatch(ids, comb, plc, tok, cot):
    width = tok.shape[1]
    vmem = pl.BlockSpec(memory_space=pltpu.VMEM)
    hbm = pl.BlockSpec(memory_space=pl.ANY)
    row_shape = jax.ShapeDtypeStruct((PLANE, ROWS, width), BF16)
    dma = pltpu.SemaphoreType.DMA
    return pl.pallas_call(
        dispatch_kernel,
        name="dispatch",
        out_shape=(row_shape, row_shape, jax.ShapeDtypeStruct((RINGS, 8, 128), F32)),
        in_specs=[vmem] * 5,
        out_specs=(hbm, hbm, vmem),
        scratch_shapes=[
            pltpu.VMEM((512, width), BF16),
            pltpu.VMEM((512, width), BF16),
            pltpu.VMEM((PLANE * ROWS, 512), BF16),
            pltpu.VMEM((PLANE * ROWS, 1), F32),
            pltpu.VMEM((PLANE, ROWS, width), BF16),
            pltpu.VMEM((PLANE, ROWS, width), BF16),
            dma((3,)), dma((3,)), dma((4, 3)), dma((4, 3)), dma((4,)), dma((4, 15)), dma((4, 15)),
        ],
        compiler_params=pltpu.CompilerParams(
            collective_id=0, has_side_effects=True, vmem_limit_bytes=48 * 2**20
        ),
    )(ids, comb, plc, tok, cot)


def finish_kernel(
    eo, rg, meta, moved, g0, g1, g2, o0, o1, o2, mixed, input_grad, s0, s1, s2,
    ret, whi, wlo, pick, acc, part, own, gath,
    x0, x1, x2, y0, y1, y2, r0, r1, r2,
    x_send, x_recv, y_send, y_recv, own_sem, p_send, p_recv, b_send, b_recv,
):
    p, l, y = place()
    width = mixed.shape[1]
    tokens = mixed.shape[0]
    ring = [ring_peer(p, l, y, d) for d in range(1, RINGS)]
    peers = [plane_peer(p, l, y, r) for r in range(1, PLANE)]
    across = (1 - p, y * PLANE + l)
    ready = greet(ring + [d for d, _ in peers] + [across])
    grads = [(g0, o0, x0, y0, r0, s0), (g1, o1, x1, y1, r1, s1), (g2, o2, x2, y2, r2, s2)]

    ready()
    x_copies, y_copies = [], []
    sources = (eo, rg)
    back = [[], []]
    for which in range(2):
        for r, (device, j) in enumerate(peers):
            copy = remote(
                sources[which].at[j], ret.at[which, l], p_send.at[which, r], p_recv.at[which, r], device
            )
            back[which].append(copy)
        own_copy = pltpu.make_async_copy(sources[which].at[l], ret.at[which, l], own_sem.at[which])
        back[which].append(own_copy)
    for c in range(6):
        _, other, xr, _, _, _ = grads[c // 2]
        rows = other.shape[0] // 2
        at = pl.ds((c % 2) * rows, rows)
        x_copies.append(remote(other.at[at], xr.at[at], x_send.at[c], x_recv.at[c], across))
    for copy in back[0] + x_copies + back[1]:
        copy.start()
    for b in range(RINGS):
        hit, weight = selection(meta, y * PLANE * ROWS, b)
        cols = slice(b * tokens, (b + 1) * tokens)
        high = weight.astype(BF16)
        pick[:, cols] = hit.astype(BF16)
        whi[:, cols] = high
        wlo[:, cols] = (weight - high.astype(F32)).astype(BF16)

    own_rows = pl.ds(pl.multiple_of(y * tokens, tokens), tokens)
    summed = [[], []]

    def combine(which):
        for r, copy in enumerate(back[which]):
            if r < PLANE - 1:
                copy.wait_recv()
            else:
                copy.wait()

        def step(n, _):
            at = columns(n)
            rows = ret[which, :, :, at].reshape(PLANE * ROWS, TILE)
            if which == 0:
                total = lax.dot_general(whi[...], rows, CONTRACT_ROWS, preferred_element_type=F32)
                total += lax.dot_general(wlo[...], rows, CONTRACT_ROWS, preferred_element_type=F32)
            else:
                total = lax.dot_general(pick[...], rows, CONTRACT_ROWS, preferred_element_type=F32)
            acc[:, at] = total
            part[which, :, at] = total.astype(BF16)
            return 0

        lax.fori_loop(0, width // TILE, step, 0)
        own[which] = acc[own_rows, :]
        for d in range(3):
            there = pl.ds(pl.multiple_of(lax.rem(y + d + 1, RINGS) * tokens, tokens), tokens)
            copy = remote(
                part.at[which, there, :], gath.at[which, d], b_send.at[which, d], b_recv.at[which, d], ring[d]
            )
            copy.start()
            summed[which].append(copy)

    for c in range(6):
        mine, other, xr, ys, yr, _ = grads[c // 2]
        rows = other.shape[0] // 2
        at = pl.ds((c % 2) * rows, rows)
        x_copies[c].wait_recv()
        ys[at, :] = (0.5 * (mine[at, :] + xr[at, :].astype(F32))).astype(BF16)
        copy = remote(ys.at[at], yr.at[at], y_send.at[c], y_recv.at[c], ring[1])
        copy.start()
        y_copies.append(copy)
        if c == 1:
            combine(0)
        if c == 3:
            combine(1)
    for which, out in enumerate((mixed, input_grad)):
        total = own[which]
        for d in range(3):
            summed[which][d].wait_recv()
            total += gath[which, d].astype(F32)
        out[...] = total.astype(BF16)
    for c in range(6):
        _, other, _, ys, yr, out = grads[c // 2]
        rows = other.shape[0] // 2
        at = pl.ds((c % 2) * rows, rows)
        y_copies[c].wait_recv()
        out[at, :] = jnp.where(moved[0:1, 0:1] > 0.0, yr[at, :].astype(F32), ys[at, :].astype(F32)).astype(BF16)
    for copy in back[0][:-1] + back[1][:-1] + x_copies + y_copies + summed[0] + summed[1]:
        copy.wait_send()


def finish(eo, rg, meta, moved, own, other):
    width = eo.shape[-1]
    vmem = pl.BlockSpec(memory_space=pltpu.VMEM)
    hbm = pl.BlockSpec(memory_space=pl.ANY)
    dma = pltpu.SemaphoreType.DMA
    row_shape = jax.ShapeDtypeStruct((128, width), BF16)
    slabs = [pltpu.VMEM(o.shape, BF16) for o in other]
    return pl.pallas_call(
        finish_kernel,
        name="finish",
        out_shape=(row_shape, row_shape) + tuple(jax.ShapeDtypeStruct(o.shape, BF16) for o in other),
        in_specs=[hbm, hbm, vmem, vmem] + [vmem] * 3 + [hbm] * 3,
        out_specs=(vmem,) * 5,
        scratch_shapes=[
            pltpu.VMEM((2, PLANE, ROWS, width), BF16),
            pltpu.VMEM((PLANE * ROWS, 512), BF16),
            pltpu.VMEM((PLANE * ROWS, 512), BF16),
            pltpu.VMEM((PLANE * ROWS, 512), BF16),
            pltpu.VMEM((512, width), F32),
            pltpu.VMEM((2, 512, width), BF16),
            pltpu.VMEM((2, 128, width), F32),
            pltpu.VMEM((2, 3, 128, width), BF16),
        ]
        + slabs * 3
        + [dma((6,)), dma((6,)), dma((6,)), dma((6,)), dma((2,)), dma((2, 15)), dma((2, 15)), dma((2, 3)), dma((2, 3))],
        compiler_params=pltpu.CompilerParams(
            collective_id=1, has_side_effects=True, vmem_limit_bytes=62 * 2**20
        ),
    )(eo, rg, meta, moved, *own, *other)


def body(tokens, cotangent, expert_ids, combine, placement, moves, w_gate, w_up, w_down):
    gate_weight, up_weight, down_weight = w_gate[0], w_up[0], w_down[0]
    width, ff = gate_weight.shape
    p = lax.axis_index("dp")
    my_move = jnp.sum(jnp.where(jnp.arange(moves.shape[0]) == lax.axis_index("expert"), moves, 0))
    moved = jnp.broadcast_to(my_move.astype(F32), (8, 128))
    x, og, meta = dispatch(expert_ids.T, combine.T, placement[:, None], tokens, cotangent)
    row_inputs = x.reshape(PLANE * ROWS, width)
    out_grad = og.reshape(PLANE * ROWS, width)
    gate_pre = jnp.dot(row_inputs, gate_weight, preferred_element_type=F32)
    up_pre = jnp.dot(row_inputs, up_weight, preferred_element_type=F32)
    sigma = jax.nn.sigmoid(gate_pre)
    hidden = (gate_pre * sigma * up_pre).astype(BF16)
    expert_out = jnp.dot(hidden, down_weight, preferred_element_type=F32).astype(BF16)
    hidden_grad = lax.dot_general(out_grad, down_weight, CONTRACT_LAST, preferred_element_type=F32)
    gate_grad = (hidden_grad * up_pre * sigma * (1.0 + gate_pre * (1.0 - sigma))).astype(BF16)
    up_grad = (hidden_grad * gate_pre * sigma).astype(BF16)
    row_grad = (
        lax.dot_general(gate_grad, gate_weight, CONTRACT_LAST, preferred_element_type=F32)
        + lax.dot_general(up_grad, up_weight, CONTRACT_LAST, preferred_element_type=F32)
    ).astype(BF16)

    def halves(left, right):
        size = left.shape[1] // 2
        mine = lax.dynamic_slice_in_dim(left, p * size, size, 1)
        other = lax.dynamic_slice_in_dim(left, (1 - p) * size, size, 1)
        return (
            lax.dot_general(mine, right, CONTRACT_ROWS, preferred_element_type=F32),
            lax.dot_general(other, right, CONTRACT_ROWS, preferred_element_type=F32).astype(BF16),
        )

    pairs = [halves(row_inputs, gate_grad), halves(row_inputs, up_grad), halves(hidden, out_grad)]
    mixed, input_grad, *grads = finish(
        expert_out.reshape(PLANE, ROWS, width),
        row_grad.reshape(PLANE, ROWS, width),
        meta,
        moved,
        [a for a, _ in pairs],
        [b for _, b in pairs],
    )
    return (mixed, input_grad) + tuple(g.astype(F32)[None] for g in grads)


def solution(mesh):
    tok = P(("dp", "expert"), None)
    weight = P("expert", None, None)
    grad = P("expert", "dp", None)
    return jax.shard_map(
        body,
        mesh=mesh,
        in_specs=(tok, tok, tok, tok, P(), P(), weight, weight, weight),
        out_specs=(tok, tok, grad, grad, grad),
        check_vma=False,
    )
```

```python
import jax
import jax.numpy as jnp
from jax import lax
from jax.experimental import pallas as pl
from jax.experimental.pallas import tpu as pltpu
from jax.sharding import PartitionSpec as P

MESH = pl.DeviceIdType.MESH
BF16 = jnp.bfloat16
F32 = jnp.float32
PLANE = 16
RINGS = 4
CAP = 12
ROWS = RINGS * CAP
TILE = 256
CONTRACT_ROWS = (((0,), (0,)), ((), ()))
CONTRACT_LAST = (((1,), (1,)), ((), ()))


def place():
    p = lax.axis_index("dp")
    e = lax.axis_index("expert")
    return p, lax.rem(e, PLANE), e // PLANE


def plane_peer(p, l, y, r):
    rc, rx, rz = r % 2, (r // 2) % 2, r // 4
    core, xh, z = lax.rem(l, 2), lax.rem(l // 2, 2), l // 4
    j = lax.rem(z + rz, 4) * 4 + lax.rem(xh + rx, 2) * 2 + lax.rem(core + rc, 2)
    return (p if rx == 0 else 1 - p, y * PLANE + j), j


def plane_source(p, l, y, r):
    rc, rx, rz = r % 2, (r // 2) % 2, r // 4
    core, xh, z = lax.rem(l, 2), lax.rem(l // 2, 2), l // 4
    j = lax.rem(z + 4 - rz, 4) * 4 + lax.rem(xh + rx, 2) * 2 + lax.rem(core + rc, 2)
    return (p if rx == 0 else 1 - p, y * PLANE + j), j


def ring_peer(p, l, y, d):
    return (p, lax.rem(y + d, RINGS) * PLANE + l)


def remote(src, dst, send, recv, device):
    return pltpu.make_async_remote_copy(
        src_ref=src, dst_ref=dst, send_sem=send, recv_sem=recv, device_id=device, device_id_type=MESH
    )


def greet(devices):
    barrier = pltpu.get_barrier_semaphore()
    for device in devices:
        pl.semaphore_signal(barrier, inc=1, device_id=device, device_id_type=MESH)
    return lambda: pl.semaphore_wait(barrier, len(devices))


def columns(n):
    return pl.ds(pl.multiple_of(n * TILE, TILE), TILE)


def selection(meta, base, ring):
    m = meta[ring]
    row = (lax.broadcasted_iota(jnp.int32, (PLANE * ROWS, 128), 0) + base).astype(F32)
    hit = jnp.zeros((PLANE * ROWS, 128), F32)
    weight = jnp.zeros((PLANE * ROWS, 128), F32)
    for k in range(4):
        same = row == m[k : k + 1, :]
        hit = jnp.where(same, 1.0, hit)
        weight = jnp.where(same, m[4 + k : 5 + k, :], weight)
    return hit, weight


def load(src, dst, sem):
    copy = pltpu.make_async_copy(src, dst, sem)
    copy.start()
    return copy


def dispatch_kernel(
    ids, comb, plc, tok, cot, wg, wu, wd, x_out, og_out, meta, pre_out, hid_out, eo_out,
    gtok, gcot, pick, rw, sx, so, x, wgu, wdv, pre, hid, eo,
    meta_send, meta_recv, ag_send, ag_recv, own_sem, d_send, d_recv, w_sem, out_sem,
):
    p, l, y = place()
    width = tok.shape[1]
    ff = wg.shape[1]
    half = width // 2
    ring = [ring_peer(p, l, y, d) for d in range(1, RINGS)]
    peers = [plane_peer(p, l, y, r) for r in range(1, PLANE)]
    ready = greet(ring + [d for d, _ in peers])
    weights = [
        load(wg, wgu.at[:, pl.ds(0, ff)], w_sem.at[0]),
        load(wu, wgu.at[:, pl.ds(ff, ff)], w_sem.at[1]),
        load(wd, wdv, w_sem.at[2]),
    ]

    slots = plc.shape[0]
    tokens = ids.shape[1]
    slot_id = lax.broadcasted_iota(jnp.int32, (slots, tokens), 0)
    owned = [(plc[...] == ids[k : k + 1, :]) for k in range(4)]
    member = jnp.zeros((slots, tokens), F32)
    for o in owned:
        member = jnp.where(o, 1.0, member)
    before = (
        lax.broadcasted_iota(jnp.int32, (tokens, tokens), 0)
        < lax.broadcasted_iota(jnp.int32, (tokens, tokens), 1)
    ).astype(F32)
    rank = jnp.dot(member.astype(BF16), before.astype(BF16), preferred_element_type=F32)
    position = rank + (slot_id * ROWS + y * CAP).astype(F32)
    rows = [jnp.sum(jnp.where(o, position, 0.0), axis=0, keepdims=True) for o in owned]
    meta[y] = jnp.concatenate(rows + [comb[...]], axis=0)
    own_rows = pl.ds(pl.multiple_of(y * tokens, tokens), tokens)

    ready()
    copies = [
        remote(meta.at[y], meta.at[y], meta_send.at[d], meta_recv.at[d], ring[d]) for d in range(3)
    ]
    gather = []
    for c in range(4):
        src, dst = (tok, gtok) if c < 2 else (cot, gcot)
        cols = pl.ds((c % 2) * half, half)
        gather.append([
            remote(src.at[:, cols], dst.at[own_rows, cols], ag_send.at[c, d], ag_recv.at[c, d], ring[d])
            for d in range(3)
        ])
    for copy in copies + [g for group in gather for g in group]:
        copy.start()
    gtok[own_rows, :] = tok[...]
    gcot[own_rows, :] = cot[...]
    for copy in copies:
        copy.wait_recv()
    for b in range(RINGS):
        hit, weight = selection(meta, y * PLANE * ROWS, b)
        pick[:, b * tokens : (b + 1) * tokens] = hit.astype(BF16)
        total = jnp.sum(weight, axis=1, keepdims=True)
        rw[...] = total if b == 0 else rw[...] + total

    sent, own = [], []
    for c in range(4):
        src, buf, dst = (gtok, sx, x) if c < 2 else (gcot, so, og_out)
        cols = pl.ds((c % 2) * half, half)
        for copy in gather[c]:
            copy.wait_recv()

        def step(n, _, src=src, buf=buf, c=c):
            at = columns((c % 2) * (half // TILE) + n)
            got = jnp.dot(pick[...], src[:, at], preferred_element_type=F32)
            if c >= 2:
                got = rw[...] * got
            buf[:, :, at] = got.astype(BF16).reshape(PLANE, ROWS, TILE)
            return 0

        lax.fori_loop(0, half // TILE, step, 0)
        group = []
        for r, (device, j) in enumerate(peers):
            copy = remote(buf.at[j, :, cols], dst.at[l, :, cols], d_send.at[c, r], d_recv.at[c, r], device)
            copy.start()
            group.append(copy)
        sent.append(group)
        own.append(load(buf.at[l, :, cols], dst.at[l, :, cols], own_sem.at[c]))

    for c in range(2):
        own[c].wait()
        for copy in sent[c]:
            copy.wait_recv()
    outs = [load(x, x_out, out_sem.at[0])]
    for copy in weights:
        copy.wait()

    def forward(n, _):
        gate_at = columns(n)
        up_at = columns(ff // TILE + n)
        rows = x[...].reshape(PLANE * ROWS, width)
        gate = jnp.dot(rows, wgu[:, gate_at], preferred_element_type=F32)
        up = jnp.dot(rows, wgu[:, up_at], preferred_element_type=F32)
        pre[:, gate_at] = gate
        pre[:, up_at] = up
        hid[:, gate_at] = (gate * jax.nn.sigmoid(gate) * up).astype(BF16)
        return 0

    lax.fori_loop(0, ff // TILE, forward, 0)
    outs.append(load(pre, pre_out, out_sem.at[1]))
    outs.append(load(hid, hid_out, out_sem.at[2]))

    def project(n, _):
        at = columns(n)
        got = jnp.dot(hid[...], wdv[:, at], preferred_element_type=F32)
        eo[:, :, at] = got.astype(BF16).reshape(PLANE, ROWS, TILE)
        return 0

    lax.fori_loop(0, width // TILE, project, 0)
    outs.append(load(eo, eo_out, out_sem.at[3]))
    for c in range(2, 4):
        own[c].wait()
        for copy in sent[c]:
            copy.wait_recv()
    for copy in outs:
        copy.wait()
    for copy in copies + [g for group in gather + sent for g in group]:
        copy.wait_send()


def dispatch(ids, comb, plc, tok, cot, wg, wu, wd):
    width = tok.shape[1]
    ff = wg.shape[1]
    rows = PLANE * ROWS
    vmem = pl.BlockSpec(memory_space=pltpu.VMEM)
    hbm = pl.BlockSpec(memory_space=pl.ANY)
    row_shape = jax.ShapeDtypeStruct((PLANE, ROWS, width), BF16)
    row_buffer = pltpu.VMEM((PLANE, ROWS, width), BF16)
    dma = pltpu.SemaphoreType.DMA
    return pl.pallas_call(
        dispatch_kernel,
        name="dispatch",
        out_shape=(
            row_shape,
            row_shape,
            jax.ShapeDtypeStruct((RINGS, 8, 128), F32),
            jax.ShapeDtypeStruct((rows, 2 * ff), F32),
            jax.ShapeDtypeStruct((rows, ff), BF16),
            row_shape,
        ),
        in_specs=[vmem] * 5 + [hbm] * 3,
        out_specs=(hbm, hbm, vmem, hbm, hbm, hbm),
        scratch_shapes=[
            pltpu.VMEM((512, width), BF16),
            pltpu.VMEM((512, width), BF16),
            pltpu.VMEM((rows, 512), BF16),
            pltpu.VMEM((rows, 1), F32),
            row_buffer,
            row_buffer,
            row_buffer,
            pltpu.VMEM((width, 2 * ff), BF16),
            pltpu.VMEM((ff, width), BF16),
            pltpu.VMEM((rows, 2 * ff), F32),
            pltpu.VMEM((rows, ff), BF16),
            row_buffer,
            dma((3,)), dma((3,)), dma((4, 3)), dma((4, 3)), dma((4,)), dma((4, 15)), dma((4, 15)),
            dma((3,)), dma((4,)),
        ],
        compiler_params=pltpu.CompilerParams(
            collective_id=0, has_side_effects=True, vmem_limit_bytes=60 * 2**20
        ),
    )(ids, comb, plc, tok, cot, wg, wu, wd)


DOWN = 128
WIDE = 256
NARROW = 128


def finish_kernel(
    x_in, og_in, eo, pre_in, hid_in, meta, wg, wu, wd,
    mixed, input_grad, own_down, own_wide, got_down, got_wide,
    x, og, pre, hid, wgu, wdv, gu, rg, ret, whi, wlo, pick, acc, part, own, gath, fresh,
    oth_down, oth_wide, x_down, x_wide,
    in_sem, x_send, x_recv, y_send, y_recv, s_sem, own_sem, p_send, p_recv, b_send, b_recv,
):
    p, l, y = place()
    tokens, width = mixed.shape
    ff = hid.shape[1]
    rows_all = PLANE * ROWS
    ring = [ring_peer(p, l, y, d) for d in range(1, RINGS)]
    peers = [plane_peer(p, l, y, r) for r in range(1, PLANE)]
    across = (1 - p, y * PLANE + l)
    ready = greet(ring + [d for d, _ in peers] + [across])
    loads = [
        load(hid_in, hid, in_sem.at[0]),
        load(og_in, og, in_sem.at[1]),
        load(wd, wdv, in_sem.at[2]),
        load(pre_in, pre, in_sem.at[3]),
        load(x_in, x, in_sem.at[4]),
        load(wg, wgu.at[:, pl.ds(0, ff)], in_sem.at[5]),
        load(wu, wgu.at[:, pl.ds(ff, ff)], in_sem.at[6]),
    ]
    downs = (ff // 2) // DOWN
    narrows = (width // 2) // NARROW
    chunks = downs + narrows

    def slab(c, down, wide):
        if c < downs:
            return down.at[pl.ds(c * DOWN, DOWN)]
        return wide.at[pl.ds((c - downs) * NARROW, NARROW)]

    def down_part(side, c):
        at = pl.ds(pl.multiple_of(side * (ff // 2) + c * DOWN, DOWN), DOWN)
        return lambda cols: lax.dot_general(
            hid[:, at], og[:, :, cols].reshape(rows_all, -1), CONTRACT_ROWS, preferred_element_type=F32
        )

    def wide_part(side, c):
        at = pl.ds(pl.multiple_of(side * (width // 2) + c * WIDE, WIDE), WIDE)
        return lambda cols: lax.dot_general(
            x[:, :, at].reshape(rows_all, WIDE), gu[:, cols], CONTRACT_ROWS, preferred_element_type=F32
        )

    back = [[], []]
    for which, source in enumerate((eo, rg)):
        for r, (device, j) in enumerate(peers):
            back[which].append(
                remote(source.at[j], ret.at[which, l], p_send.at[which, r], p_recv.at[which, r], device)
            )
        back[which].append(pltpu.make_async_copy(source.at[l], ret.at[which, l], own_sem.at[which]))
    x_copies = [
        remote(slab(c, oth_down, oth_wide), slab(c, x_down, x_wide), x_send.at[c], x_recv.at[c], across)
        for c in range(chunks)
    ]
    y_copies = [
        remote(slab(c, x_down, x_wide), slab(c, got_down, got_wide), y_send.at[c], y_recv.at[c], ring[1])
        for c in range(chunks)
    ]
    kept = [
        pltpu.make_async_copy(slab(c, x_down, x_wide), slab(c, own_down, own_wide), s_sem.at[c])
        for c in range(chunks)
    ]

    ready()
    loads[0].wait()
    loads[1].wait()
    for c in range(downs):
        part_of = down_part(1 - p, c)
        for n in range(width // 512):
            cols = slice(n * 512, (n + 1) * 512)
            oth_down[c * DOWN : (c + 1) * DOWN, cols] = (0.5 * part_of(cols)).astype(BF16)
        x_copies[c].start()
        if c == 0:
            for copy in back[0]:
                copy.start()
    loads[2].wait()
    loads[3].wait()

    def backward(n, _):
        gate_at = columns(n)
        up_at = columns(ff // TILE + n)
        grad = lax.dot_general(
            og[...].reshape(rows_all, width), wdv[gate_at, :], CONTRACT_LAST, preferred_element_type=F32
        )
        gate, up = pre[:, gate_at], pre[:, up_at]
        sigma = jax.nn.sigmoid(gate)
        gu[:, gate_at] = (grad * up * sigma * (1.0 + gate * (1.0 - sigma))).astype(BF16)
        gu[:, up_at] = (grad * gate * sigma).astype(BF16)
        return 0

    lax.fori_loop(0, ff // TILE, backward, 0)
    loads[4].wait()
    per = WIDE // NARROW
    for c in range(narrows // per):
        part_of = wide_part(1 - p, c)
        for n in range(2):
            cols = slice(n * ff, (n + 1) * ff)
            oth_wide[c * WIDE : (c + 1) * WIDE, cols] = (0.5 * part_of(cols)).astype(BF16)
        for i in range(per):
            x_copies[downs + c * per + i].start()
    loads[5].wait()
    loads[6].wait()

    def pull(n, _):
        at = columns(n)
        got = lax.dot_general(gu[...], wgu[at, :], CONTRACT_LAST, preferred_element_type=F32)
        rg[:, :, at] = got.astype(BF16).reshape(PLANE, ROWS, TILE)
        return 0

    lax.fori_loop(0, width // TILE, pull, 0)
    for copy in back[1]:
        copy.start()
    for b in range(RINGS):
        hit, weight = selection(meta, y * PLANE * ROWS, b)
        cols = slice(b * tokens, (b + 1) * tokens)
        high = weight.astype(BF16)
        pick[:, cols] = hit.astype(BF16)
        whi[:, cols] = high
        wlo[:, cols] = (weight - high.astype(F32)).astype(BF16)

    own_rows = pl.ds(pl.multiple_of(y * tokens, tokens), tokens)
    summed = [[], []]

    def combine(which):
        for copy in back[which][:-1]:
            copy.wait_recv()
        back[which][-1].wait()

        def step(n, _):
            at = columns(n)
            rows = ret[which, :, :, at].reshape(rows_all, TILE)
            if which == 0:
                total = lax.dot_general(whi[...], rows, CONTRACT_ROWS, preferred_element_type=F32)
                total += lax.dot_general(wlo[...], rows, CONTRACT_ROWS, preferred_element_type=F32)
            else:
                total = lax.dot_general(pick[...], rows, CONTRACT_ROWS, preferred_element_type=F32)
            acc[...] = total
            part[which, :, at] = total.astype(BF16)
            own[which, :, at] = acc[own_rows, :]
            return 0

        lax.fori_loop(0, width // TILE, step, 0)
        for d in range(3):
            there = pl.ds(pl.multiple_of(lax.rem(y + d + 1, RINGS) * tokens, tokens), tokens)
            copy = remote(
                part.at[which, there, :], gath.at[which, d], b_send.at[which, d], b_recv.at[which, d], ring[d]
            )
            copy.start()
            summed[which].append(copy)

    for c in range(chunks):
        if c < downs:
            part_of = down_part(p, c)
            at = slice(c * DOWN, (c + 1) * DOWN)
            x_copies[c].wait_recv()
            for n in range(width // 512):
                cols = slice(n * 512, (n + 1) * 512)
                x_down[at, cols] = (0.5 * part_of(cols) + x_down[at, cols].astype(F32)).astype(BF16)
        else:
            i = c - downs
            if i % per == 0:
                part_of = wide_part(p, i // per)
                for n in range(2):
                    cols = slice(n * ff, (n + 1) * ff)
                    fresh[:, cols] = 0.5 * part_of(cols)
            at = slice(i * NARROW, (i + 1) * NARROW)
            x_copies[c].wait_recv()
            mine = fresh[(i % per) * NARROW : (i % per + 1) * NARROW, :]
            x_wide[at, :] = (mine + x_wide[at, :].astype(F32)).astype(BF16)
        y_copies[c].start()
        kept[c].start()
        if c == EARLY:
            combine(0)
        if c == LATE:
            combine(1)
    for which, out in enumerate((mixed, input_grad)):
        total = own[which]
        for d in range(3):
            summed[which][d].wait_recv()
            total += gath[which, d].astype(F32)
        out[...] = total.astype(BF16)
    for c in range(chunks):
        y_copies[c].wait()
        kept[c].wait()
    for copy in back[0][:-1] + back[1][:-1] + x_copies + summed[0] + summed[1]:
        copy.wait_send()


EARLY = 2
LATE = 7


def finish(x, og, eo, pre, hid, meta, wg, wu, wd):
    width = x.shape[-1]
    ff = hid.shape[1]
    rows = PLANE * ROWS
    vmem = pl.BlockSpec(memory_space=pltpu.VMEM)
    hbm = pl.BlockSpec(memory_space=pl.ANY)
    dma = pltpu.SemaphoreType.DMA
    chunks = (ff // 2) // DOWN + (width // 2) // NARROW
    row_shape = jax.ShapeDtypeStruct((128, width), BF16)
    row_buffer = pltpu.VMEM((PLANE, ROWS, width), BF16)
    down_shape, wide_shape = (ff // 2, width), (width // 2, 2 * ff)
    grads = [jax.ShapeDtypeStruct(s, BF16) for s in (down_shape, wide_shape)]
    slabs = [pltpu.VMEM(s, BF16) for s in (down_shape, wide_shape)]
    return pl.pallas_call(
        finish_kernel,
        name="finish",
        out_shape=(row_shape, row_shape, *grads, *grads),
        in_specs=[hbm] * 5 + [vmem] + [hbm] * 3,
        out_specs=(vmem, vmem, hbm, hbm, hbm, hbm),
        scratch_shapes=[
            row_buffer,
            row_buffer,
            pltpu.VMEM((rows, 2 * ff), F32),
            pltpu.VMEM((rows, ff), BF16),
            pltpu.VMEM((width, 2 * ff), BF16),
            pltpu.VMEM((ff, width), BF16),
            pltpu.VMEM((rows, 2 * ff), BF16),
            row_buffer,
            pltpu.VMEM((2, PLANE, ROWS, width), BF16),
            pltpu.VMEM((rows, 512), BF16),
            pltpu.VMEM((rows, 512), BF16),
            pltpu.VMEM((rows, 512), BF16),
            pltpu.VMEM((512, TILE), F32),
            pltpu.VMEM((2, 512, width), BF16),
            pltpu.VMEM((2, 128, width), F32),
            pltpu.VMEM((2, 3, 128, width), BF16),
            pltpu.VMEM((WIDE, 2 * ff), F32),
            *slabs,
            *slabs,
            dma((7,)), dma((chunks,)), dma((chunks,)), dma((chunks,)), dma((chunks,)), dma((chunks,)),
            dma((2,)), dma((2, 15)), dma((2, 15)), dma((2, 3)), dma((2, 3)),
        ],
        compiler_params=pltpu.CompilerParams(
            collective_id=1, has_side_effects=True, vmem_limit_bytes=63 * 2**20
        ),
    )(x, og, eo, pre, hid, meta, wg, wu, wd)


def body(tokens, cotangent, expert_ids, combine, placement, moves, w_gate, w_up, w_down):
    weights = (w_gate[0], w_up[0], w_down[0])
    ff = weights[0].shape[1]
    mine = jnp.arange(moves.shape[0]) == lax.axis_index("expert")
    moved = jnp.sum(jnp.where(mine, moves, 0)) > 0
    x, og, meta, pre, hid, eo = dispatch(
        expert_ids.T, combine.T, placement[:, None], tokens, cotangent, *weights
    )
    mixed, input_grad, own_down, own_wide, got_down, got_wide = finish(
        x, og, eo, pre, hid, meta, *weights
    )
    down = jnp.where(moved, got_down, own_down).astype(F32)
    gate = jnp.where(moved, got_wide[:, :ff], own_wide[:, :ff]).astype(F32)
    up = jnp.where(moved, got_wide[:, ff:], own_wide[:, ff:]).astype(F32)
    return mixed, input_grad, gate[None], up[None], down[None]


def solution(mesh):
    tok = P(("dp", "expert"), None)
    weight = P("expert", None, None)
    grad = P("expert", "dp", None)
    return jax.shard_map(
        body,
        mesh=mesh,
        in_specs=(tok, tok, tok, tok, P(), P(), weight, weight, weight),
        out_specs=(tok, tok, grad, grad, grad),
        check_vma=False,
    )
```

```python
import jax
import jax.numpy as jnp
from jax import lax
from jax.experimental import pallas as pl
from jax.experimental.pallas import tpu as pltpu
from jax.sharding import PartitionSpec as P

MESH = pl.DeviceIdType.MESH
BF16 = jnp.bfloat16
F32 = jnp.float32
PLANE = 16
RINGS = 4
CAP = 12
ROWS = RINGS * CAP
TILE = 256
CONTRACT_ROWS = (((0,), (0,)), ((), ()))
CONTRACT_LAST = (((1,), (1,)), ((), ()))


def place():
    p = lax.axis_index("dp")
    e = lax.axis_index("expert")
    return p, lax.rem(e, PLANE), e // PLANE


def plane_peer(p, l, y, r):
    rc, rx, rz = r % 2, (r // 2) % 2, r // 4
    core, xh, z = lax.rem(l, 2), lax.rem(l // 2, 2), l // 4
    j = lax.rem(z + rz, 4) * 4 + lax.rem(xh + rx, 2) * 2 + lax.rem(core + rc, 2)
    return (p if rx == 0 else 1 - p, y * PLANE + j), j


def plane_source(p, l, y, r):
    rc, rx, rz = r % 2, (r // 2) % 2, r // 4
    core, xh, z = lax.rem(l, 2), lax.rem(l // 2, 2), l // 4
    j = lax.rem(z + 4 - rz, 4) * 4 + lax.rem(xh + rx, 2) * 2 + lax.rem(core + rc, 2)
    return (p if rx == 0 else 1 - p, y * PLANE + j), j


def ring_peer(p, l, y, d):
    return (p, lax.rem(y + d, RINGS) * PLANE + l)


def remote(src, dst, send, recv, device):
    return pltpu.make_async_remote_copy(
        src_ref=src, dst_ref=dst, send_sem=send, recv_sem=recv, device_id=device, device_id_type=MESH
    )


def greet(devices):
    barrier = pltpu.get_barrier_semaphore()
    for device in devices:
        pl.semaphore_signal(barrier, inc=1, device_id=device, device_id_type=MESH)
    return lambda: pl.semaphore_wait(barrier, len(devices))


def columns(n):
    return pl.ds(pl.multiple_of(n * TILE, TILE), TILE)


def selection(meta, base, ring):
    m = meta[ring]
    row = (lax.broadcasted_iota(jnp.int32, (PLANE * ROWS, 128), 0) + base).astype(F32)
    hit = jnp.zeros((PLANE * ROWS, 128), F32)
    weight = jnp.zeros((PLANE * ROWS, 128), F32)
    for k in range(4):
        same = row == m[k : k + 1, :]
        hit = jnp.where(same, 1.0, hit)
        weight = jnp.where(same, m[4 + k : 5 + k, :], weight)
    return hit, weight


def moving(table, p, l, y):
    slot = lax.broadcasted_iota(jnp.int32, (table.shape[0], 1), 0)
    mine = jnp.where(slot == y * PLANE + l, table[:, 1:2], 0)
    return jnp.sum(mine.astype(F32), axis=0, keepdims=True) > 0.0


def load(src, dst, sem):
    copy = pltpu.make_async_copy(src, dst, sem)
    copy.start()
    return copy


def dispatch_kernel(
    ids, comb, table, tok, cot, wg, wu, wd,
    x_out, og_out, meta, pre_out, hid_out, eo_out, wgu_out, wd_out,
    gtok, gcot, pick, rw, sx, so, x, wgu, wdv, pre, hid, eo, new_wide, new_down,
    meta_send, meta_recv, ag_send, ag_recv, own_sem, d_send, d_recv, w_sem, out_sem,
    swap_send, swap_recv, pass_send, pass_recv,
):
    p, l, y = place()
    width = tok.shape[1]
    ff = wg.shape[1]
    half = width // 2
    ring = [ring_peer(p, l, y, d) for d in range(1, RINGS)]
    peers = [plane_peer(p, l, y, r) for r in range(1, PLANE)]
    across = (1 - p, y * PLANE + l)
    ready = greet(ring + [d for d, _ in peers] + [across])
    odd = lax.rem(l, 2) == 1
    wide_half, down_half = width // 2, ff // 2
    wide_rows = pl.ds(pl.multiple_of(p * wide_half, wide_half), wide_half)
    down_rows = pl.ds(pl.multiple_of(p * down_half, down_half), down_half)
    whole = [
        pltpu.make_async_copy(wg, wgu.at[:, pl.ds(0, ff)], w_sem.at[0]),
        pltpu.make_async_copy(wu, wgu.at[:, pl.ds(ff, ff)], w_sem.at[1]),
        pltpu.make_async_copy(wd, wdv, w_sem.at[2]),
    ]
    partly = [
        pltpu.make_async_copy(wg.at[wide_rows], wgu.at[wide_rows, pl.ds(0, ff)], w_sem.at[0]),
        pltpu.make_async_copy(wu.at[wide_rows], wgu.at[wide_rows, pl.ds(ff, ff)], w_sem.at[1]),
        pltpu.make_async_copy(wd.at[down_rows], wdv.at[down_rows], w_sem.at[2]),
    ]
    swaps, passes, pieces = [], [], []
    for i in range(6):
        which = i // 2
        size = (wide_half if which < 2 else down_half) // 2
        source = (wg, wu, wd)[which]
        at = pl.ds(pl.multiple_of(p * 2 * size + (i % 2) * size, size), size)
        near = pl.ds((i % 2) * size, size)
        if which < 2:
            landed = new_wide.at[near, pl.ds(which * ff, ff)]
            held = wgu.at[at, pl.ds(which * ff, ff)]
        else:
            landed = new_down.at[near]
            held = wdv.at[at]
        swaps.append(remote(source.at[at], landed, swap_send.at[i], swap_recv.at[i], ring[1]))
        passes.append(remote(held, held, pass_send.at[i], pass_recv.at[i], across))
        pieces.append((landed, held, size))

    @pl.when(odd)
    def _():
        for copy in partly:
            copy.start()

    @pl.when(jnp.logical_not(odd))
    def _():
        for copy in whole:
            copy.start()

    slots = table.shape[0]
    tokens = ids.shape[1]
    slot_id = lax.broadcasted_iota(jnp.int32, (slots, tokens), 0)
    plc, moves = table[:, 0:1], table[:, 1:2]
    paired = jnp.concatenate([plc[slots // 2 :], plc[: slots // 2]], axis=0)
    one = lax.broadcasted_iota(jnp.int32, (slots, 1), 0)
    located = jnp.where((lax.rem(one, 2) == 1) & (moves == 1), paired, plc)
    owned = [(located == ids[k : k + 1, :]) for k in range(4)]
    member = jnp.zeros((slots, tokens), F32)
    for o in owned:
        member = jnp.where(o, 1.0, member)
    before = (
        lax.broadcasted_iota(jnp.int32, (tokens, tokens), 0)
        < lax.broadcasted_iota(jnp.int32, (tokens, tokens), 1)
    ).astype(F32)
    rank = jnp.dot(member.astype(BF16), before.astype(BF16), preferred_element_type=F32)
    position = rank + (slot_id * ROWS + y * CAP).astype(F32)
    rows = [jnp.sum(jnp.where(o, position, 0.0), axis=0, keepdims=True) for o in owned]
    meta[y] = jnp.concatenate(rows + [comb[...]], axis=0)
    own_rows = pl.ds(pl.multiple_of(y * tokens, tokens), tokens)

    ready()
    copies = [
        remote(meta.at[y], meta.at[y], meta_send.at[d], meta_recv.at[d], ring[d]) for d in range(3)
    ]
    gather = []
    for c in range(4):
        src, dst = (tok, gtok) if c < 2 else (cot, gcot)
        cols = pl.ds((c % 2) * half, half)
        gather.append([
            remote(src.at[:, cols], dst.at[own_rows, cols], ag_send.at[c, d], ag_recv.at[c, d], ring[d])
            for d in range(3)
        ])
    for copy in copies + [g for group in gather for g in group]:
        copy.start()
    gtok[own_rows, :] = tok[...]
    gcot[own_rows, :] = cot[...]
    for copy in copies:
        copy.wait_recv()
    for b in range(RINGS):
        hit, weight = selection(meta, y * PLANE * ROWS, b)
        pick[:, b * tokens : (b + 1) * tokens] = hit.astype(BF16)
        total = jnp.sum(weight, axis=1, keepdims=True)
        rw[...] = total if b == 0 else rw[...] + total

    sent, own = [], []
    for c in range(4):
        src, buf, dst = (gtok, sx, x) if c < 2 else (gcot, so, og_out)
        cols = pl.ds((c % 2) * half, half)
        for copy in gather[c]:
            copy.wait_recv()
        if c == 2:

            @pl.when(odd)
            def _():
                for copy in swaps:
                    copy.start()

        def step(n, _, src=src, buf=buf, c=c):
            at = columns((c % 2) * (half // TILE) + n)
            got = jnp.dot(pick[...], src[:, at], preferred_element_type=F32)
            if c >= 2:
                got = rw[...] * got
            buf[:, :, at] = got.astype(BF16).reshape(PLANE, ROWS, TILE)
            return 0

        lax.fori_loop(0, half // TILE, step, 0)
        group = []
        for r, (device, j) in enumerate(peers):
            copy = remote(buf.at[j, :, cols], dst.at[l, :, cols], d_send.at[c, r], d_recv.at[c, r], device)
            copy.start()
            group.append(copy)
        sent.append(group)
        own.append(load(buf.at[l, :, cols], dst.at[l, :, cols], own_sem.at[c]))

    for c in range(2):
        own[c].wait()
        for copy in sent[c]:
            copy.wait_recv()
    outs = [load(x, x_out, out_sem.at[0])]

    @pl.when(jnp.logical_not(odd))
    def _():
        for copy in whole:
            copy.wait()

    @pl.when(odd)
    def _():
        for copy in partly:
            copy.wait()
        take = moving(table, p, l, y)
        for i, (landed, held, size) in enumerate(pieces):
            swaps[i].wait_recv()
            held[...] = jnp.where(take, landed[...].astype(F32), held[...].astype(F32)).astype(BF16)
            passes[i].start()
        for copy in passes[:4]:
            copy.wait_recv()

    outs.append(load(wgu, wgu_out, out_sem.at[4]))

    def forward(n, _):
        gate_at = columns(n)
        up_at = columns(ff // TILE + n)
        rows = x[...].reshape(PLANE * ROWS, width)
        gate = jnp.dot(rows, wgu[:, gate_at], preferred_element_type=F32)
        up = jnp.dot(rows, wgu[:, up_at], preferred_element_type=F32)
        pre[:, gate_at] = gate
        pre[:, up_at] = up
        hid[:, gate_at] = (gate * jax.nn.sigmoid(gate) * up).astype(BF16)
        return 0

    lax.fori_loop(0, ff // TILE, forward, 0)
    outs.append(load(pre, pre_out, out_sem.at[1]))
    outs.append(load(hid, hid_out, out_sem.at[2]))

    @pl.when(odd)
    def _():
        for copy in passes[4:]:
            copy.wait_recv()

    outs.append(load(wdv, wd_out, out_sem.at[5]))

    def project(n, _):
        at = columns(n)
        got = jnp.dot(hid[...], wdv[:, at], preferred_element_type=F32)
        eo[:, :, at] = got.astype(BF16).reshape(PLANE, ROWS, TILE)
        return 0

    lax.fori_loop(0, width // TILE, project, 0)
    outs.append(load(eo, eo_out, out_sem.at[3]))
    for c in range(2, 4):
        own[c].wait()
        for copy in sent[c]:
            copy.wait_recv()
    for copy in outs:
        copy.wait()
    for copy in copies + [g for group in gather + sent for g in group]:
        copy.wait_send()

    @pl.when(odd)
    def _():
        for copy in swaps + passes:
            copy.wait_send()


def dispatch(ids, comb, table, tok, cot, wg, wu, wd):
    width = tok.shape[1]
    ff = wg.shape[1]
    rows = PLANE * ROWS
    vmem = pl.BlockSpec(memory_space=pltpu.VMEM)
    hbm = pl.BlockSpec(memory_space=pl.ANY)
    row_shape = jax.ShapeDtypeStruct((PLANE, ROWS, width), BF16)
    row_buffer = pltpu.VMEM((PLANE, ROWS, width), BF16)
    dma = pltpu.SemaphoreType.DMA
    return pl.pallas_call(
        dispatch_kernel,
        name="dispatch",
        out_shape=(
            row_shape,
            row_shape,
            jax.ShapeDtypeStruct((RINGS, 8, 128), F32),
            jax.ShapeDtypeStruct((rows, 2 * ff), F32),
            jax.ShapeDtypeStruct((rows, ff), BF16),
            row_shape,
            jax.ShapeDtypeStruct((width, 2 * ff), BF16),
            jax.ShapeDtypeStruct((ff, width), BF16),
        ),
        in_specs=[vmem] * 5 + [hbm] * 3,
        out_specs=(hbm, hbm, vmem, hbm, hbm, hbm, hbm, hbm),
        scratch_shapes=[
            pltpu.VMEM((512, width), BF16),
            pltpu.VMEM((512, width), BF16),
            pltpu.VMEM((rows, 512), BF16),
            pltpu.VMEM((rows, 1), F32),
            row_buffer,
            row_buffer,
            row_buffer,
            pltpu.VMEM((width, 2 * ff), BF16),
            pltpu.VMEM((ff, width), BF16),
            pltpu.VMEM((rows, 2 * ff), F32),
            pltpu.VMEM((rows, ff), BF16),
            row_buffer,
            pltpu.VMEM((width // 2, 2 * ff), BF16),
            pltpu.VMEM((ff // 2, width), BF16),
            dma((3,)), dma((3,)), dma((4, 3)), dma((4, 3)), dma((4,)), dma((4, 15)), dma((4, 15)),
            dma((3,)), dma((6,)), dma((6,)), dma((6,)), dma((6,)), dma((6,)),
        ],
        compiler_params=pltpu.CompilerParams(
            collective_id=0, has_side_effects=True, vmem_limit_bytes=60 * 2**20
        ),
    )(ids, comb, table, tok, cot, wg, wu, wd)


DOWN = 128
WIDE = 256
NARROW = 128


def finish_kernel(
    x_in, og_in, eo, pre_in, hid_in, meta, table, wgu_in, wd_in,
    mixed, input_grad, own_down, own_wide,
    x, og, pre, hid, wgu, wdv, gu, rg, ret, whi, wlo, pick, acc, part, own, gath,
    oth_down, oth_wide, x_down, x_wide, got_down, got_wide,
    in_sem, x_send, x_recv, y_send, y_recv, s_sem, own_sem, p_send, p_recv, b_send, b_recv,
):
    p, l, y = place()
    tokens, width = mixed.shape
    ff = hid.shape[1]
    rows_all = PLANE * ROWS
    ring = [ring_peer(p, l, y, d) for d in range(1, RINGS)]
    peers = [plane_peer(p, l, y, r) for r in range(1, PLANE)]
    across = (1 - p, y * PLANE + l)
    ready = greet(ring + [d for d, _ in peers] + [across])
    loads = [
        load(hid_in, hid, in_sem.at[0]),
        load(og_in, og, in_sem.at[1]),
        load(wd_in, wdv, in_sem.at[2]),
        load(pre_in, pre, in_sem.at[3]),
        load(x_in, x, in_sem.at[4]),
        load(wgu_in, wgu, in_sem.at[5]),
    ]
    even = lax.rem(l, 2) == 0
    fresh = pre
    downs = (ff // 2) // DOWN
    narrows = (width // 2) // NARROW
    chunks = downs + narrows

    def slab(c, down, wide):
        if c < downs:
            return down.at[pl.ds(c * DOWN, DOWN)]
        return wide.at[pl.ds((c - downs) * NARROW, NARROW)]

    def down_part(side, c):
        at = pl.ds(pl.multiple_of(side * (ff // 2) + c * DOWN, DOWN), DOWN)
        return lambda cols: lax.dot_general(
            hid[:, at], og[:, :, cols].reshape(rows_all, -1), CONTRACT_ROWS, preferred_element_type=F32
        )

    def wide_part(side, c):
        at = pl.ds(pl.multiple_of(side * (width // 2) + c * WIDE, WIDE), WIDE)
        return lambda cols: lax.dot_general(
            x[:, :, at].reshape(rows_all, WIDE), gu[:, cols], CONTRACT_ROWS, preferred_element_type=F32
        )

    back = [[], []]
    for which, source in enumerate((eo, rg)):
        for r, (device, j) in enumerate(peers):
            back[which].append(
                remote(source.at[j], ret.at[which, l], p_send.at[which, r], p_recv.at[which, r], device)
            )
        back[which].append(pltpu.make_async_copy(source.at[l], ret.at[which, l], own_sem.at[which]))
    x_copies = [
        remote(slab(c, oth_down, oth_wide), slab(c, x_down, x_wide), x_send.at[c], x_recv.at[c], across)
        for c in range(chunks)
    ]
    y_copies = [
        remote(slab(c, x_down, x_wide), slab(c, got_down, got_wide), y_send.at[c], y_recv.at[c], ring[1])
        for c in range(chunks)
    ]
    kept = [
        pltpu.make_async_copy(slab(c, x_down, x_wide), slab(c, own_down, own_wide), s_sem.at[c])
        for c in range(chunks)
    ]

    ready()
    loads[0].wait()
    loads[1].wait()
    for c in range(downs):
        part_of = down_part(1 - p, c)
        for n in range(width // 512):
            cols = slice(n * 512, (n + 1) * 512)
            oth_down[c * DOWN : (c + 1) * DOWN, cols] = (0.5 * part_of(cols)).astype(BF16)
        pl.when(even)(x_copies[c].start)
        if c == 0:
            for copy in back[0]:
                copy.start()
    loads[2].wait()
    loads[3].wait()

    def backward(n, _):
        gate_at = columns(n)
        up_at = columns(ff // TILE + n)
        grad = lax.dot_general(
            og[...].reshape(rows_all, width), wdv[gate_at, :], CONTRACT_LAST, preferred_element_type=F32
        )
        gate, up = pre[:, gate_at], pre[:, up_at]
        sigma = jax.nn.sigmoid(gate)
        gu[:, gate_at] = (grad * up * sigma * (1.0 + gate * (1.0 - sigma))).astype(BF16)
        gu[:, up_at] = (grad * gate * sigma).astype(BF16)
        return 0

    lax.fori_loop(0, ff // TILE, backward, 0)
    loads[4].wait()
    per = WIDE // NARROW
    for c in range(narrows // per):
        part_of = wide_part(1 - p, c)
        for n in range(2):
            cols = slice(n * ff, (n + 1) * ff)
            oth_wide[c * WIDE : (c + 1) * WIDE, cols] = (0.5 * part_of(cols)).astype(BF16)
        for i in range(per):
            pl.when(even)(x_copies[downs + c * per + i].start)
    loads[5].wait()

    def pull(n, _):
        at = columns(n)
        got = lax.dot_general(gu[...], wgu[at, :], CONTRACT_LAST, preferred_element_type=F32)
        rg[:, :, at] = got.astype(BF16).reshape(PLANE, ROWS, TILE)
        return 0

    lax.fori_loop(0, width // TILE, pull, 0)
    for copy in back[1]:
        copy.start()
    for b in range(RINGS):
        hit, weight = selection(meta, y * PLANE * ROWS, b)
        cols = slice(b * tokens, (b + 1) * tokens)
        high = weight.astype(BF16)
        pick[:, cols] = hit.astype(BF16)
        whi[:, cols] = high
        wlo[:, cols] = (weight - high.astype(F32)).astype(BF16)

    own_rows = pl.ds(pl.multiple_of(y * tokens, tokens), tokens)
    summed = [[], []]

    def combine(which):
        for copy in back[which][:-1]:
            copy.wait_recv()
        back[which][-1].wait()

        def step(n, _):
            at = columns(n)
            rows = ret[which, :, :, at].reshape(rows_all, TILE)
            if which == 0:
                total = lax.dot_general(whi[...], rows, CONTRACT_ROWS, preferred_element_type=F32)
                total += lax.dot_general(wlo[...], rows, CONTRACT_ROWS, preferred_element_type=F32)
            else:
                total = lax.dot_general(pick[...], rows, CONTRACT_ROWS, preferred_element_type=F32)
            acc[...] = total
            part[which, :, at] = total.astype(BF16)
            own[which, :, at] = acc[own_rows, :]
            return 0

        lax.fori_loop(0, width // TILE, step, 0)
        for d in range(3):
            there = pl.ds(pl.multiple_of(lax.rem(y + d + 1, RINGS) * tokens, tokens), tokens)
            copy = remote(
                part.at[which, there, :], gath.at[which, d], b_send.at[which, d], b_recv.at[which, d], ring[d]
            )
            copy.start()
            summed[which].append(copy)

    def reduce(c):
        if c < downs:
            part_of = down_part(p, c)
            at = slice(c * DOWN, (c + 1) * DOWN)
            x_copies[c].wait_recv()
            for n in range(width // 512):
                cols = slice(n * 512, (n + 1) * 512)
                x_down[at, cols] = (0.5 * part_of(cols) + x_down[at, cols].astype(F32)).astype(BF16)
        else:
            i = c - downs
            if i % per == 0:
                part_of = wide_part(p, i // per)
                for n in range(2):
                    cols = slice(n * ff, (n + 1) * ff)
                    fresh[0:WIDE, cols] = 0.5 * part_of(cols)
            at = slice(i * NARROW, (i + 1) * NARROW)
            x_copies[c].wait_recv()
            mine = fresh[(i % per) * NARROW : (i % per + 1) * NARROW, :]
            x_wide[at, :] = (mine + x_wide[at, :].astype(F32)).astype(BF16)

    @pl.when(even)
    def _():
        for c in range(EARLY):
            reduce(c)
            y_copies[c].start()

    combine(0)

    @pl.when(even)
    def _():
        for c in range(EARLY, chunks):
            reduce(c)
            y_copies[c].start()

    @pl.when(jnp.logical_not(even))
    def _():
        for copy in x_copies:
            copy.start()

    combine(1)

    @pl.when(even)
    def _():
        take = moving(table, p, l, y)
        for c in range(chunks):
            y_copies[c].wait()
            mine, got = slab(c, x_down, x_wide), slab(c, got_down, got_wide)
            mine[...] = jnp.where(take, got[...].astype(F32), mine[...].astype(F32)).astype(BF16)
            kept[c].start()

    @pl.when(jnp.logical_not(even))
    def _():
        for c in range(chunks):
            reduce(c)
            kept[c].start()

    for which, out in enumerate((mixed, input_grad)):
        total = own[which]
        for d in range(3):
            summed[which][d].wait_recv()
            total += gath[which, d].astype(F32)
        out[...] = total.astype(BF16)
    for copy in kept:
        copy.wait()
    for copy in back[0][:-1] + back[1][:-1] + x_copies + summed[0] + summed[1]:
        copy.wait_send()


EARLY = 8


def finish(x, og, eo, pre, hid, meta, table, wgu, wd):
    width = x.shape[-1]
    ff = hid.shape[1]
    rows = PLANE * ROWS
    vmem = pl.BlockSpec(memory_space=pltpu.VMEM)
    hbm = pl.BlockSpec(memory_space=pl.ANY)
    dma = pltpu.SemaphoreType.DMA
    chunks = (ff // 2) // DOWN + (width // 2) // NARROW
    row_shape = jax.ShapeDtypeStruct((128, width), BF16)
    row_buffer = pltpu.VMEM((PLANE, ROWS, width), BF16)
    down_shape, wide_shape = (ff // 2, width), (width // 2, 2 * ff)
    grads = [jax.ShapeDtypeStruct(s, BF16) for s in (down_shape, wide_shape)]
    slabs = [pltpu.VMEM(s, BF16) for s in (down_shape, wide_shape)]
    return pl.pallas_call(
        finish_kernel,
        name="finish",
        out_shape=(row_shape, row_shape, *grads),
        in_specs=[hbm] * 5 + [vmem] * 2 + [hbm] * 2,
        out_specs=(vmem, vmem, hbm, hbm),
        scratch_shapes=[
            row_buffer,
            row_buffer,
            pltpu.VMEM((rows, 2 * ff), F32),
            pltpu.VMEM((rows, ff), BF16),
            pltpu.VMEM((width, 2 * ff), BF16),
            pltpu.VMEM((ff, width), BF16),
            pltpu.VMEM((rows, 2 * ff), BF16),
            row_buffer,
            pltpu.VMEM((2, PLANE, ROWS, width), BF16),
            pltpu.VMEM((rows, 512), BF16),
            pltpu.VMEM((rows, 512), BF16),
            pltpu.VMEM((rows, 512), BF16),
            pltpu.VMEM((512, TILE), F32),
            pltpu.VMEM((2, 512, width), BF16),
            pltpu.VMEM((2, 128, width), F32),
            pltpu.VMEM((2, 3, 128, width), BF16),
            *slabs,
            *slabs,
            *slabs,
            dma((6,)), dma((chunks,)), dma((chunks,)), dma((chunks,)), dma((chunks,)), dma((chunks,)),
            dma((2,)), dma((2, 15)), dma((2, 15)), dma((2, 3)), dma((2, 3)),
        ],
        compiler_params=pltpu.CompilerParams(
            collective_id=1, has_side_effects=True, vmem_limit_bytes=63 * 2**20
        ),
    )(x, og, eo, pre, hid, meta, table, wgu, wd)


def body(tokens, cotangent, expert_ids, combine, placement, moves, w_gate, w_up, w_down):
    weights = (w_gate[0], w_up[0], w_down[0])
    ff = weights[0].shape[1]
    table = jnp.stack([placement, moves], axis=1)
    x, og, meta, pre, hid, eo, wgu, wd = dispatch(
        expert_ids.T, combine.T, table, tokens, cotangent, *weights
    )
    mixed, input_grad, down, wide = finish(x, og, eo, pre, hid, meta, table, wgu, wd)
    gate, up = wide[:, :ff], wide[:, ff:]
    return (mixed, input_grad) + tuple(g.astype(F32)[None] for g in (gate, up, down))


def solution(mesh):
    tok = P(("dp", "expert"), None)
    weight = P("expert", None, None)
    grad = P("expert", "dp", None)
    return jax.shard_map(
        body,
        mesh=mesh,
        in_specs=(tok, tok, tok, tok, P(), P(), weight, weight, weight),
        out_specs=(tok, tok, grad, grad, grad),
        check_vma=False,
    )
```

```python
import jax
import jax.numpy as jnp
from jax import lax
from jax.experimental import pallas as pl
from jax.experimental.pallas import tpu as pltpu
from jax.sharding import PartitionSpec as P

MESH = pl.DeviceIdType.MESH
BF16 = jnp.bfloat16
F32 = jnp.float32
PLANE = 16
RINGS = 4
CAP = 12
ROWS = RINGS * CAP
TILE = 256
CONTRACT_ROWS = (((0,), (0,)), ((), ()))
CONTRACT_LAST = (((1,), (1,)), ((), ()))


def place():
    p = lax.axis_index("dp")
    e = lax.axis_index("expert")
    return p, lax.rem(e, PLANE), e // PLANE


def plane_peer(p, l, y, r):
    rc, rx, rz = r % 2, (r // 2) % 2, r // 4
    core, xh, z = lax.rem(l, 2), lax.rem(l // 2, 2), l // 4
    j = lax.rem(z + rz, 4) * 4 + lax.rem(xh + rx, 2) * 2 + lax.rem(core + rc, 2)
    return (p if rx == 0 else 1 - p, y * PLANE + j), j


def plane_source(p, l, y, r):
    rc, rx, rz = r % 2, (r // 2) % 2, r // 4
    core, xh, z = lax.rem(l, 2), lax.rem(l // 2, 2), l // 4
    j = lax.rem(z + 4 - rz, 4) * 4 + lax.rem(xh + rx, 2) * 2 + lax.rem(core + rc, 2)
    return (p if rx == 0 else 1 - p, y * PLANE + j), j


def ring_peer(p, l, y, d):
    return (p, lax.rem(y + d, RINGS) * PLANE + l)


def remote(src, dst, send, recv, device):
    return pltpu.make_async_remote_copy(
        src_ref=src, dst_ref=dst, send_sem=send, recv_sem=recv, device_id=device, device_id_type=MESH
    )


def greet(devices):
    barrier = pltpu.get_barrier_semaphore()
    for device in devices:
        pl.semaphore_signal(barrier, inc=1, device_id=device, device_id_type=MESH)
    return lambda: pl.semaphore_wait(barrier, len(devices))


def columns(n):
    return pl.ds(pl.multiple_of(n * TILE, TILE), TILE)


def selection(meta, base, ring):
    m = meta[ring]
    row = (lax.broadcasted_iota(jnp.int32, (PLANE * ROWS, 128), 0) + base).astype(F32)
    hit = jnp.zeros((PLANE * ROWS, 128), F32)
    weight = jnp.zeros((PLANE * ROWS, 128), F32)
    for k in range(4):
        same = row == m[k : k + 1, :]
        hit = jnp.where(same, 1.0, hit)
        weight = jnp.where(same, m[4 + k : 5 + k, :], weight)
    return hit, weight


def moving(table, p, l, y):
    slot = lax.broadcasted_iota(jnp.int32, (table.shape[0], 1), 0)
    mine = jnp.where(slot == y * PLANE + l, table[:, 1:2], 0)
    return jnp.sum(mine.astype(F32), axis=0, keepdims=True) > 0.0


def load(src, dst, sem):
    copy = pltpu.make_async_copy(src, dst, sem)
    copy.start()
    return copy


PIECES = 4


def dispatch_kernel(
    ids, comb, table, tok, cot, wg, wu, wd,
    x_out, og_out, meta, pre_out, hid_out, wgu_out, wd_out, eo_out,
    gtok, gcot, pick, rw, sx, so, x, wgu, wdv, pre, hid, new_wide, new_down, eo,
    meta_send, meta_recv, ag_send, ag_recv, own_sem, d_send, d_recv, w_sem, out_sem,
    swap_send, swap_recv, pass_send, pass_recv,
):
    p, l, y = place()
    width = tok.shape[1]
    ff = wg.shape[1]
    half = width // 2
    ring = [ring_peer(p, l, y, d) for d in range(1, RINGS)]
    peers = [plane_peer(p, l, y, r) for r in range(1, PLANE)]
    across = (1 - p, y * PLANE + l)
    ready = greet(ring + [d for d, _ in peers] + [across])
    odd = lax.rem(l, 2) == 1
    wide_half, down_half = width // 2, ff // 2
    wide_rows = pl.ds(pl.multiple_of(p * wide_half, wide_half), wide_half)
    down_rows = pl.ds(pl.multiple_of(p * down_half, down_half), down_half)
    whole = [
        pltpu.make_async_copy(wg, wgu.at[:, pl.ds(0, ff)], w_sem.at[0]),
        pltpu.make_async_copy(wu, wgu.at[:, pl.ds(ff, ff)], w_sem.at[1]),
        pltpu.make_async_copy(wd, wdv, w_sem.at[2]),
    ]
    partly = [
        pltpu.make_async_copy(wg.at[wide_rows], wgu.at[wide_rows, pl.ds(0, ff)], w_sem.at[0]),
        pltpu.make_async_copy(wu.at[wide_rows], wgu.at[wide_rows, pl.ds(ff, ff)], w_sem.at[1]),
        pltpu.make_async_copy(wd.at[down_rows], wdv.at[down_rows], w_sem.at[2]),
    ]
    swaps, passes, pieces = [], [], []
    for i in range(3 * PIECES):
        which, piece = i // PIECES, i % PIECES
        size = (wide_half if which < 2 else down_half) // PIECES
        source = (wg, wu, wd)[which]
        at = pl.ds(pl.multiple_of(p * PIECES * size + piece * size, size), size)
        near = pl.ds(piece * size, size)
        if which < 2:
            landed = new_wide.at[near, pl.ds(which * ff, ff)]
            held = wgu.at[at, pl.ds(which * ff, ff)]
        else:
            landed = new_down.at[near]
            held = wdv.at[at]
        swaps.append(remote(source.at[at], landed, swap_send.at[i], swap_recv.at[i], ring[1]))
        passes.append(remote(held, held, pass_send.at[i], pass_recv.at[i], across))
        pieces.append((landed, held))

    take = moving(table, p, l, y)

    def settle(i):
        landed, held = pieces[i]
        swaps[i].wait_recv()
        held[...] = jnp.where(take, landed[...].astype(F32), held[...].astype(F32)).astype(BF16)
        passes[i].start()

    @pl.when(odd)
    def _():
        for copy in partly:
            copy.start()

    @pl.when(jnp.logical_not(odd))
    def _():
        for copy in whole:
            copy.start()

    slots = table.shape[0]
    tokens = ids.shape[1]
    slot_id = lax.broadcasted_iota(jnp.int32, (slots, tokens), 0)
    plc, moves = table[:, 0:1], table[:, 1:2]
    paired = jnp.concatenate([plc[slots // 2 :], plc[: slots // 2]], axis=0)
    one = lax.broadcasted_iota(jnp.int32, (slots, 1), 0)
    located = jnp.where((lax.rem(one, 2) == 1) & (moves == 1), paired, plc)
    owned = [(located == ids[k : k + 1, :]) for k in range(4)]
    member = jnp.zeros((slots, tokens), F32)
    for o in owned:
        member = jnp.where(o, 1.0, member)
    before = (
        lax.broadcasted_iota(jnp.int32, (tokens, tokens), 0)
        < lax.broadcasted_iota(jnp.int32, (tokens, tokens), 1)
    ).astype(F32)
    rank = jnp.dot(member.astype(BF16), before.astype(BF16), preferred_element_type=F32)
    position = rank + (slot_id * ROWS + y * CAP).astype(F32)
    rows = [jnp.sum(jnp.where(o, position, 0.0), axis=0, keepdims=True) for o in owned]
    meta[y] = jnp.concatenate(rows + [comb[...]], axis=0)
    own_rows = pl.ds(pl.multiple_of(y * tokens, tokens), tokens)

    ready()
    copies = [
        remote(meta.at[y], meta.at[y], meta_send.at[d], meta_recv.at[d], ring[d]) for d in range(3)
    ]
    gather = []
    for c in range(4):
        src, dst = (tok, gtok) if c < 2 else (cot, gcot)
        cols = pl.ds((c % 2) * half, half)
        gather.append([
            remote(src.at[:, cols], dst.at[own_rows, cols], ag_send.at[c, d], ag_recv.at[c, d], ring[d])
            for d in range(3)
        ])
    for copy in copies + [g for group in gather for g in group]:
        copy.start()
    gtok[own_rows, :] = tok[...]
    gcot[own_rows, :] = cot[...]
    for copy in copies:
        copy.wait_recv()
    for b in range(RINGS):
        hit, weight = selection(meta, y * PLANE * ROWS, b)
        pick[:, b * tokens : (b + 1) * tokens] = hit.astype(BF16)
        total = jnp.sum(weight, axis=1, keepdims=True)
        rw[...] = total if b == 0 else rw[...] + total

    sent, own = [], []
    for c in range(4):
        src, buf, dst = (gtok, sx, x) if c < 2 else (gcot, so, og_out)
        cols = pl.ds((c % 2) * half, half)
        for copy in gather[c]:
            copy.wait_recv()
        if c == 1:

            @pl.when(odd)
            def _():
                for copy in swaps:
                    copy.start()

        def step(n, _, src=src, buf=buf, c=c):
            at = columns((c % 2) * (half // TILE) + n)
            got = jnp.dot(pick[...], src[:, at], preferred_element_type=F32)
            if c >= 2:
                got = rw[...] * got
            buf[:, :, at] = got.astype(BF16).reshape(PLANE, ROWS, TILE)
            return 0

        lax.fori_loop(0, half // TILE, step, 0)
        group = []
        for r, (device, j) in enumerate(peers):
            copy = remote(buf.at[j, :, cols], dst.at[l, :, cols], d_send.at[c, r], d_recv.at[c, r], device)
            copy.start()
            group.append(copy)
        sent.append(group)
        if c >= 2:

            @pl.when(odd)
            def _(c=c):
                if c == 2:
                    for copy in partly:
                        copy.wait()
                for i in range(2 * (c - 2), 2 * (c - 1)):
                    settle(i)

        own.append(load(buf.at[l, :, cols], dst.at[l, :, cols], own_sem.at[c]))

    for c in range(2):
        own[c].wait()
        for copy in sent[c]:
            copy.wait_recv()
    outs = [load(x, x_out, out_sem.at[0])]

    @pl.when(jnp.logical_not(odd))
    def _():
        for copy in whole:
            copy.wait()

    @pl.when(odd)
    def _():
        for i in range(4, 2 * PIECES):
            settle(i)
        for copy in passes[: 2 * PIECES]:
            copy.wait_recv()

    outs.append(load(wgu, wgu_out, out_sem.at[3]))
    for n in range(ff // TILE):
        gate_at = slice(n * TILE, (n + 1) * TILE)
        up_at = slice(ff + n * TILE, ff + (n + 1) * TILE)
        rows = x[...].reshape(PLANE * ROWS, width)
        gate = jnp.dot(rows, wgu[:, gate_at], preferred_element_type=F32)
        up = jnp.dot(rows, wgu[:, up_at], preferred_element_type=F32)
        pre[:, gate_at] = gate
        pre[:, up_at] = up
        hid[:, gate_at] = (gate * jax.nn.sigmoid(gate) * up).astype(BF16)

        @pl.when(odd)
        def _(n=n):
            settle(2 * PIECES + n)

    outs.append(load(pre, pre_out, out_sem.at[1]))
    outs.append(load(hid, hid_out, out_sem.at[2]))

    @pl.when(odd)
    def _():
        for i in range(2 * PIECES + ff // TILE, 3 * PIECES):
            settle(i)
        for copy in passes[2 * PIECES :]:
            copy.wait_recv()

    outs.append(load(wdv, wd_out, out_sem.at[4]))
    eo_copy = pltpu.make_async_copy(eo, eo_out, out_sem.at[0])

    @pl.when(jnp.logical_not(odd))
    def _():
        def project(n, _):
            at = columns(n)
            eo[:, at] = jnp.dot(hid[...], wdv[:, at], preferred_element_type=F32).astype(BF16)
            return 0

        lax.fori_loop(0, width // TILE, project, 0)
        outs[0].wait()
        eo_copy.start()

    @pl.when(odd)
    def _():
        outs[0].wait()

    for c in range(2, 4):
        own[c].wait()
        for copy in sent[c]:
            copy.wait_recv()
    for copy in outs[1:]:
        copy.wait()
    pl.when(jnp.logical_not(odd))(eo_copy.wait)
    for copy in copies + [g for group in gather + sent for g in group]:
        copy.wait_send()

    @pl.when(odd)
    def _():
        for copy in swaps + passes:
            copy.wait_send()


def dispatch(ids, comb, table, tok, cot, wg, wu, wd):
    width = tok.shape[1]
    ff = wg.shape[1]
    rows = PLANE * ROWS
    vmem = pl.BlockSpec(memory_space=pltpu.VMEM)
    hbm = pl.BlockSpec(memory_space=pl.ANY)
    row_shape = jax.ShapeDtypeStruct((PLANE, ROWS, width), BF16)
    row_buffer = pltpu.VMEM((PLANE, ROWS, width), BF16)
    dma = pltpu.SemaphoreType.DMA
    return pl.pallas_call(
        dispatch_kernel,
        name="dispatch",
        out_shape=(
            row_shape,
            row_shape,
            jax.ShapeDtypeStruct((RINGS, 8, 128), F32),
            jax.ShapeDtypeStruct((rows, 2 * ff), F32),
            jax.ShapeDtypeStruct((rows, ff), BF16),
            jax.ShapeDtypeStruct((width, 2 * ff), BF16),
            jax.ShapeDtypeStruct((ff, width), BF16),
            jax.ShapeDtypeStruct((rows, width), BF16),
        ),
        in_specs=[vmem] * 5 + [hbm] * 3,
        out_specs=(hbm, hbm, vmem, hbm, hbm, hbm, hbm, hbm),
        scratch_shapes=[
            pltpu.VMEM((512, width), BF16),
            pltpu.VMEM((512, width), BF16),
            pltpu.VMEM((rows, 512), BF16),
            pltpu.VMEM((rows, 1), F32),
            row_buffer,
            row_buffer,
            row_buffer,
            pltpu.VMEM((width, 2 * ff), BF16),
            pltpu.VMEM((ff, width), BF16),
            pltpu.VMEM((rows, 2 * ff), F32),
            pltpu.VMEM((rows, ff), BF16),
            pltpu.VMEM((width // 2, 2 * ff), BF16),
            pltpu.VMEM((ff // 2, width), BF16),
            pltpu.VMEM((rows, width), BF16),
            dma((3,)), dma((3,)), dma((4, 3)), dma((4, 3)), dma((4,)), dma((4, 15)), dma((4, 15)),
            dma((3,)), dma((5,)), *[dma((3 * PIECES,)) for _ in range(4)],
        ],
        compiler_params=pltpu.CompilerParams(
            collective_id=0, has_side_effects=True, vmem_limit_bytes=60 * 2**20
        ),
    )(ids, comb, table, tok, cot, wg, wu, wd)


DOWN = 128
WIDE = 256
NARROW = 128


def finish_kernel(
    x_in, og_in, pre_in, hid_in, meta, table, wgu_in, wd_in, eo_in,
    mixed, input_grad, own_down, own_wide,
    x, og, pre, hid, wgu, wdv, gu, rg, ret, whi, wlo, pick, acc, part, own, gath,
    oth_down, oth_wide, x_down, x_wide, got_down, got_wide,
    in_sem, x_send, x_recv, y_send, y_recv, s_sem, own_sem, p_send, p_recv, b_send, b_recv,
):
    p, l, y = place()
    tokens, width = mixed.shape
    ff = hid.shape[1]
    rows_all = PLANE * ROWS
    ring = [ring_peer(p, l, y, d) for d in range(1, RINGS)]
    peers = [plane_peer(p, l, y, r) for r in range(1, PLANE)]
    across = (1 - p, y * PLANE + l)
    ready = greet(ring + [d for d, _ in peers] + [across])
    loads = [
        load(hid_in, hid, in_sem.at[0]),
        load(og_in, og, in_sem.at[1]),
        load(wd_in, wdv, in_sem.at[2]),
        load(pre_in, pre, in_sem.at[3]),
        load(x_in, x, in_sem.at[4]),
        load(wgu_in, wgu, in_sem.at[5]),
    ]
    even = lax.rem(l, 2) == 0
    eo_copy = pltpu.make_async_copy(eo_in, part.at[pl.ds(0, rows_all)], in_sem.at[6])
    pl.when(even)(eo_copy.start)
    fresh = pre
    downs = (ff // 2) // DOWN
    narrows = (width // 2) // NARROW
    chunks = downs + narrows

    def slab(c, down, wide):
        if c < downs:
            return down.at[pl.ds(c * DOWN, DOWN)]
        return wide.at[pl.ds((c - downs) * NARROW, NARROW)]

    def down_part(side, c):
        at = pl.ds(pl.multiple_of(side * (ff // 2) + c * DOWN, DOWN), DOWN)
        return lambda cols: lax.dot_general(
            hid[:, at], og[:, :, cols].reshape(rows_all, -1), CONTRACT_ROWS, preferred_element_type=F32
        )

    def wide_part(side, c):
        at = pl.ds(pl.multiple_of(side * (width // 2) + c * WIDE, WIDE), WIDE)
        return lambda cols: lax.dot_general(
            x[:, :, at].reshape(rows_all, WIDE), gu[:, cols], CONTRACT_ROWS, preferred_element_type=F32
        )

    def returned(which, j):
        if which == 0:
            return part.at[pl.ds(pl.multiple_of(j * ROWS, ROWS), ROWS)]
        return rg.at[j]

    back = [[], []]
    for which in range(2):
        for r, (device, j) in enumerate(peers):
            source = returned(which, j)
            back[which].append(
                remote(source, ret.at[which, l], p_send.at[which, r], p_recv.at[which, r], device)
            )
        back[which].append(
            pltpu.make_async_copy(returned(which, l), ret.at[which, l], own_sem.at[which])
        )
    x_copies = [
        remote(slab(c, oth_down, oth_wide), slab(c, x_down, x_wide), x_send.at[c], x_recv.at[c], across)
        for c in range(chunks)
    ]
    y_copies = [
        remote(slab(c, x_down, x_wide), slab(c, got_down, got_wide), y_send.at[c], y_recv.at[c], ring[1])
        for c in range(chunks)
    ]
    kept = [
        pltpu.make_async_copy(slab(c, x_down, x_wide), slab(c, own_down, own_wide), s_sem.at[c])
        for c in range(chunks)
    ]

    def project(n, _):
        at = columns(n)
        got = jnp.dot(hid[...], wdv[:, at], preferred_element_type=F32)
        part[0:rows_all, at] = got.astype(BF16)
        return 0

    ready()

    @pl.when(even)
    def _():
        eo_copy.wait()
        for copy in back[0]:
            copy.start()

    loads[0].wait()
    loads[1].wait()
    for c in range(downs):
        part_of = down_part(1 - p, c)
        for n in range(width // 512):
            cols = slice(n * 512, (n + 1) * 512)
            oth_down[c * DOWN : (c + 1) * DOWN, cols] = (0.5 * part_of(cols)).astype(BF16)
        pl.when(even)(x_copies[c].start)
        if c == 0:
            loads[2].wait()

            @pl.when(jnp.logical_not(even))
            def _():
                lax.fori_loop(0, width // TILE, project, 0)
                for copy in back[0]:
                    copy.start()

    loads[3].wait()

    def backward(n, _):
        gate_at = columns(n)
        up_at = columns(ff // TILE + n)
        grad = lax.dot_general(
            og[...].reshape(rows_all, width), wdv[gate_at, :], CONTRACT_LAST, preferred_element_type=F32
        )
        gate, up = pre[:, gate_at], pre[:, up_at]
        sigma = jax.nn.sigmoid(gate)
        gu[:, gate_at] = (grad * up * sigma * (1.0 + gate * (1.0 - sigma))).astype(BF16)
        gu[:, up_at] = (grad * gate * sigma).astype(BF16)
        return 0

    lax.fori_loop(0, ff // TILE, backward, 0)
    loads[4].wait()
    per = WIDE // NARROW
    for c in range(narrows // per):
        part_of = wide_part(1 - p, c)
        for n in range(2):
            cols = slice(n * ff, (n + 1) * ff)
            oth_wide[c * WIDE : (c + 1) * WIDE, cols] = (0.5 * part_of(cols)).astype(BF16)
        for i in range(per):
            pl.when(even)(x_copies[downs + c * per + i].start)
    loads[5].wait()

    def pull(n, _):
        at = columns(n)
        got = lax.dot_general(gu[...], wgu[at, :], CONTRACT_LAST, preferred_element_type=F32)
        rg[:, :, at] = got.astype(BF16).reshape(PLANE, ROWS, TILE)
        return 0

    lax.fori_loop(0, width // TILE, pull, 0)
    for copy in back[1]:
        copy.start()
    for b in range(RINGS):
        hit, weight = selection(meta, y * PLANE * ROWS, b)
        cols = slice(b * tokens, (b + 1) * tokens)
        high = weight.astype(BF16)
        pick[:, cols] = hit.astype(BF16)
        whi[:, cols] = high
        wlo[:, cols] = (weight - high.astype(F32)).astype(BF16)

    own_rows = pl.ds(pl.multiple_of(y * tokens, tokens), tokens)
    summed = [[], []]

    def combine(which):
        for copy in back[which][:-1]:
            copy.wait_recv()
        back[which][-1].wait()
        if which == 0:
            for copy in back[0][:-1]:
                copy.wait_send()
        blocks = which * RINGS * tokens

        def step(n, _):
            at = columns(n)
            rows = ret[which, :, :, at].reshape(rows_all, TILE)
            if which == 0:
                total = lax.dot_general(whi[...], rows, CONTRACT_ROWS, preferred_element_type=F32)
                total += lax.dot_general(wlo[...], rows, CONTRACT_ROWS, preferred_element_type=F32)
            else:
                total = lax.dot_general(pick[...], rows, CONTRACT_ROWS, preferred_element_type=F32)
            acc[...] = total
            part[blocks : blocks + RINGS * tokens, at] = total.astype(BF16)
            own[which, :, at] = acc[own_rows, :]
            return 0

        lax.fori_loop(0, width // TILE, step, 0)
        for d in range(3):
            there = pl.ds(pl.multiple_of(blocks + lax.rem(y + d + 1, RINGS) * tokens, tokens), tokens)
            copy = remote(
                part.at[there], gath.at[which, d], b_send.at[which, d], b_recv.at[which, d], ring[d]
            )
            copy.start()
            summed[which].append(copy)

    def reduce(c):
        if c < downs:
            part_of = down_part(p, c)
            at = slice(c * DOWN, (c + 1) * DOWN)
            x_copies[c].wait_recv()
            for n in range(width // 512):
                cols = slice(n * 512, (n + 1) * 512)
                x_down[at, cols] = (0.5 * part_of(cols) + x_down[at, cols].astype(F32)).astype(BF16)
        else:
            i = c - downs
            if i % per == 0:
                part_of = wide_part(p, i // per)
                for n in range(2):
                    cols = slice(n * ff, (n + 1) * ff)
                    fresh[0:WIDE, cols] = 0.5 * part_of(cols)
            at = slice(i * NARROW, (i + 1) * NARROW)
            x_copies[c].wait_recv()
            mine = fresh[(i % per) * NARROW : (i % per + 1) * NARROW, :]
            x_wide[at, :] = (mine + x_wide[at, :].astype(F32)).astype(BF16)

    @pl.when(even)
    def _():
        for c in range(EARLY):
            reduce(c)
            y_copies[c].start()

    combine(0)

    @pl.when(even)
    def _():
        for c in range(EARLY, chunks):
            reduce(c)
            y_copies[c].start()

    @pl.when(jnp.logical_not(even))
    def _():
        for copy in x_copies:
            copy.start()

    combine(1)

    @pl.when(even)
    def _():
        take = moving(table, p, l, y)
        for c in range(chunks):
            y_copies[c].wait()
            mine, got = slab(c, x_down, x_wide), slab(c, got_down, got_wide)
            mine[...] = jnp.where(take, got[...].astype(F32), mine[...].astype(F32)).astype(BF16)
            kept[c].start()

    @pl.when(jnp.logical_not(even))
    def _():
        for c in range(chunks):
            reduce(c)
            kept[c].start()

    for which, out in enumerate((mixed, input_grad)):
        total = own[which]
        for d in range(3):
            summed[which][d].wait_recv()
            total += gath[which, d].astype(F32)
        out[...] = total.astype(BF16)
    for copy in kept:
        copy.wait()
    for copy in back[1][:-1] + x_copies + summed[0] + summed[1]:
        copy.wait_send()


EARLY = 8


def finish(x, og, pre, hid, meta, table, wgu, wd, eo):
    width = x.shape[-1]
    ff = hid.shape[1]
    rows = PLANE * ROWS
    vmem = pl.BlockSpec(memory_space=pltpu.VMEM)
    hbm = pl.BlockSpec(memory_space=pl.ANY)
    dma = pltpu.SemaphoreType.DMA
    chunks = (ff // 2) // DOWN + (width // 2) // NARROW
    row_shape = jax.ShapeDtypeStruct((128, width), BF16)
    row_buffer = pltpu.VMEM((PLANE, ROWS, width), BF16)
    down_shape, wide_shape = (ff // 2, width), (width // 2, 2 * ff)
    grads = [jax.ShapeDtypeStruct(s, BF16) for s in (down_shape, wide_shape)]
    slabs = [pltpu.VMEM(s, BF16) for s in (down_shape, wide_shape)]
    return pl.pallas_call(
        finish_kernel,
        name="finish",
        out_shape=(row_shape, row_shape, *grads),
        in_specs=[hbm] * 4 + [vmem] * 2 + [hbm] * 3,
        out_specs=(vmem, vmem, hbm, hbm),
        scratch_shapes=[
            row_buffer,
            row_buffer,
            pltpu.VMEM((rows, 2 * ff), F32),
            pltpu.VMEM((rows, ff), BF16),
            pltpu.VMEM((width, 2 * ff), BF16),
            pltpu.VMEM((ff, width), BF16),
            pltpu.VMEM((rows, 2 * ff), BF16),
            row_buffer,
            pltpu.VMEM((2, PLANE, ROWS, width), BF16),
            pltpu.VMEM((rows, 512), BF16),
            pltpu.VMEM((rows, 512), BF16),
            pltpu.VMEM((rows, 512), BF16),
            pltpu.VMEM((512, TILE), F32),
            pltpu.VMEM((2 * 512, width), BF16),
            pltpu.VMEM((2, 128, width), F32),
            pltpu.VMEM((2, 3, 128, width), BF16),
            *slabs,
            *slabs,
            *slabs,
            dma((7,)), dma((chunks,)), dma((chunks,)), dma((chunks,)), dma((chunks,)), dma((chunks,)),
            dma((2,)), dma((2, 15)), dma((2, 15)), dma((2, 3)), dma((2, 3)),
        ],
        compiler_params=pltpu.CompilerParams(
            collective_id=1, has_side_effects=True, vmem_limit_bytes=63 * 2**20
        ),
    )(x, og, pre, hid, meta, table, wgu, wd, eo)


def body(tokens, cotangent, expert_ids, combine, placement, moves, w_gate, w_up, w_down):
    weights = (w_gate[0], w_up[0], w_down[0])
    ff = weights[0].shape[1]
    table = jnp.stack([placement, moves], axis=1)
    x, og, meta, pre, hid, wgu, wd, eo = dispatch(
        expert_ids.T, combine.T, table, tokens, cotangent, *weights
    )
    mixed, input_grad, down, wide = finish(x, og, pre, hid, meta, table, wgu, wd, eo)
    gate, up = wide[:, :ff], wide[:, ff:]
    return (mixed, input_grad) + tuple(g.astype(F32)[None] for g in (gate, up, down))


def solution(mesh):
    tok = P(("dp", "expert"), None)
    weight = P("expert", None, None)
    grad = P("expert", "dp", None)
    return jax.shard_map(
        body,
        mesh=mesh,
        in_specs=(tok, tok, tok, tok, P(), P(), weight, weight, weight),
        out_specs=(tok, tok, grad, grad, grad),
        check_vma=False,
    )
```

```python
import jax
import jax.numpy as jnp
from jax import lax
from jax.experimental import pallas as pl
from jax.experimental.pallas import tpu as pltpu
from jax.sharding import PartitionSpec as P

MESH = pl.DeviceIdType.MESH
BF16 = jnp.bfloat16
F32 = jnp.float32
PLANE = 16
RINGS = 4
CAP = 12
ROWS = RINGS * CAP
TILE = 256
CONTRACT_LAST = (((1,), (1,)), ((), ()))


def place():
    p = lax.axis_index("dp")
    e = lax.axis_index("expert")
    return p, lax.rem(e, PLANE), e // PLANE


def plane_peer(p, l, y, r):
    rc, rx, rz = r % 2, (r // 2) % 2, r // 4
    core, xh, z = lax.rem(l, 2), lax.rem(l // 2, 2), l // 4
    j = lax.rem(z + rz, 4) * 4 + lax.rem(xh + rx, 2) * 2 + lax.rem(core + rc, 2)
    return (p if rx == 0 else 1 - p, y * PLANE + j), j


def plane_source(p, l, y, r):
    rc, rx, rz = r % 2, (r // 2) % 2, r // 4
    core, xh, z = lax.rem(l, 2), lax.rem(l // 2, 2), l // 4
    j = lax.rem(z + 4 - rz, 4) * 4 + lax.rem(xh + rx, 2) * 2 + lax.rem(core + rc, 2)
    return (p if rx == 0 else 1 - p, y * PLANE + j), j


def ring_peer(p, l, y, d):
    return (p, lax.rem(y + d, RINGS) * PLANE + l)


def remote(src, dst, send, recv, device):
    return pltpu.make_async_remote_copy(
        src_ref=src, dst_ref=dst, send_sem=send, recv_sem=recv, device_id=device, device_id_type=MESH
    )


def greet(devices):
    barrier = pltpu.get_barrier_semaphore()
    for device in devices:
        pl.semaphore_signal(barrier, inc=1, device_id=device, device_id_type=MESH)
    return lambda: pl.semaphore_wait(barrier, len(devices))


def columns(n):
    return pl.ds(pl.multiple_of(n * TILE, TILE), TILE)


def selection(meta, base, ring):
    m = meta[ring]
    row = (lax.broadcasted_iota(jnp.int32, (PLANE * ROWS, 128), 0) + base).astype(F32)
    hit = jnp.zeros((PLANE * ROWS, 128), F32)
    weight = jnp.zeros((PLANE * ROWS, 128), F32)
    for k in range(4):
        same = row == m[k : k + 1, :]
        hit = jnp.where(same, 1.0, hit)
        weight = jnp.where(same, m[4 + k : 5 + k, :], weight)
    return hit, weight


def moving(table, p, l, y):
    slot = lax.broadcasted_iota(jnp.int32, (table.shape[0], 1), 0)
    mine = jnp.where(slot == y * PLANE + l, table[:, 1:2], 0)
    return jnp.sum(mine.astype(F32), axis=0, keepdims=True) > 0.0


def load(src, dst, sem):
    copy = pltpu.make_async_copy(src, dst, sem)
    copy.start()
    return copy


PIECES = 4


def dispatch_kernel(
    ids, comb, table, tok, cot, wg, wu, wd,
    x_out, og_out, meta, pre_out, hid_out, wgu_out, wd_out, eo_out,
    gtok, gcot, pick, rw, sx, so, x, wgu, wdv, pre, hid, new_wide, new_down, eo,
    meta_send, meta_recv, ag_send, ag_recv, own_sem, d_send, d_recv, w_sem, out_sem,
    swap_send, swap_recv, pass_send, pass_recv, keep_sem,
):
    p, l, y = place()
    width = tok.shape[1]
    ff = wg.shape[1]
    half = width // 2
    ring = [ring_peer(p, l, y, d) for d in range(1, RINGS)]
    peers = [plane_peer(p, l, y, r) for r in range(1, PLANE)]
    across = (1 - p, y * PLANE + l)
    ready = greet(ring + [d for d, _ in peers] + [across])
    odd = lax.rem(l, 2) == 1
    wide_half, down_half = width // 2, ff // 2
    wide_rows = pl.ds(pl.multiple_of(p * wide_half, wide_half), wide_half)
    down_rows = pl.ds(pl.multiple_of(p * down_half, down_half), down_half)
    whole = [
        pltpu.make_async_copy(wg, wgu.at[:, pl.ds(0, ff)], w_sem.at[0]),
        pltpu.make_async_copy(wu, wgu.at[:, pl.ds(ff, ff)], w_sem.at[1]),
        pltpu.make_async_copy(wd, wdv, w_sem.at[2]),
    ]
    partly = [
        pltpu.make_async_copy(wg.at[wide_rows], wgu.at[wide_rows, pl.ds(0, ff)], w_sem.at[0]),
        pltpu.make_async_copy(wu.at[wide_rows], wgu.at[wide_rows, pl.ds(ff, ff)], w_sem.at[1]),
        pltpu.make_async_copy(wd.at[down_rows], wdv.at[down_rows], w_sem.at[2]),
    ]
    swaps, passes, pieces, keeps = [], [], [], []
    for i in range(3 * PIECES):
        which, piece = i // PIECES, i % PIECES
        size = (wide_half if which < 2 else down_half) // PIECES
        source = (wg, wu, wd)[which]
        at = pl.ds(pl.multiple_of(p * PIECES * size + piece * size, size), size)
        near = pl.ds(piece * size, size)
        if which < 2:
            landed = new_wide.at[near, pl.ds(which * ff, ff)]
            held = wgu.at[at, pl.ds(which * ff, ff)]
        else:
            landed = new_down.at[near]
            held = wdv.at[at]
        swaps.append(remote(source.at[at], landed, swap_send.at[i], swap_recv.at[i], ring[1]))
        final = held if which < 2 else wd_out.at[at]
        passes.append(remote(held, final, pass_send.at[i], pass_recv.at[i], across))
        if which == 2:
            keeps.append(pltpu.make_async_copy(held, final, keep_sem.at[piece]))
        pieces.append((landed, held))

    take = moving(table, p, l, y)

    def settle(i):
        landed, held = pieces[i]
        swaps[i].wait_recv()
        held[...] = jnp.where(take, landed[...].astype(F32), held[...].astype(F32)).astype(BF16)
        passes[i].start()
        if i >= 2 * PIECES:
            keeps[i - 2 * PIECES].start()

    @pl.when(odd)
    def _():
        for copy in partly:
            copy.start()

    @pl.when(jnp.logical_not(odd))
    def _():
        for copy in whole:
            copy.start()

    slots = table.shape[0]
    tokens = ids.shape[1]
    slot_id = lax.broadcasted_iota(jnp.int32, (slots, tokens), 0)
    plc, moves = table[:, 0:1], table[:, 1:2]
    paired = jnp.concatenate([plc[slots // 2 :], plc[: slots // 2]], axis=0)
    one = lax.broadcasted_iota(jnp.int32, (slots, 1), 0)
    located = jnp.where((lax.rem(one, 2) == 1) & (moves == 1), paired, plc)
    owned = [(located == ids[k : k + 1, :]) for k in range(4)]
    member = jnp.zeros((slots, tokens), F32)
    for o in owned:
        member = jnp.where(o, 1.0, member)
    before = (
        lax.broadcasted_iota(jnp.int32, (tokens, tokens), 0)
        < lax.broadcasted_iota(jnp.int32, (tokens, tokens), 1)
    ).astype(F32)
    rank = jnp.dot(member.astype(BF16), before.astype(BF16), preferred_element_type=F32)
    position = rank + (slot_id * ROWS + y * CAP).astype(F32)
    rows = [jnp.sum(jnp.where(o, position, 0.0), axis=0, keepdims=True) for o in owned]
    meta[y] = jnp.concatenate(rows + [comb[...]], axis=0)
    own_rows = pl.ds(pl.multiple_of(y * tokens, tokens), tokens)

    ready()
    copies = [
        remote(meta.at[y], meta.at[y], meta_send.at[d], meta_recv.at[d], ring[d]) for d in range(3)
    ]
    gather = []
    for c in range(4):
        src, dst = (tok, gtok) if c < 2 else (cot, gcot)
        cols = pl.ds((c % 2) * half, half)
        gather.append([
            remote(src.at[:, cols], dst.at[own_rows, cols], ag_send.at[c, d], ag_recv.at[c, d], ring[d])
            for d in range(3)
        ])
    for copy in copies + [g for group in gather for g in group]:
        copy.start()
    gtok[own_rows, :] = tok[...]
    gcot[own_rows, :] = cot[...]
    for copy in copies:
        copy.wait_recv()
    for b in range(RINGS):
        hit, weight = selection(meta, y * PLANE * ROWS, b)
        pick[:, b * tokens : (b + 1) * tokens] = hit.astype(BF16)
        total = jnp.sum(weight, axis=1, keepdims=True)
        rw[...] = total if b == 0 else rw[...] + total

    sent, own = [], []
    for c in range(4):
        src, buf, dst = (gtok, sx, x) if c < 2 else (gcot, so, og_out)
        cols = pl.ds((c % 2) * half, half)
        for copy in gather[c]:
            copy.wait_recv()
        if c == 1:

            @pl.when(odd)
            def _():
                for copy in swaps:
                    copy.start()

        def step(n, _, src=src, buf=buf, c=c):
            at = columns((c % 2) * (half // TILE) + n)
            got = jnp.dot(pick[...], src[:, at], preferred_element_type=F32)
            if c >= 2:
                got = rw[...] * got
            buf[:, :, at] = got.astype(BF16).reshape(PLANE, ROWS, TILE)
            return 0

        lax.fori_loop(0, half // TILE, step, 0)
        group = []
        for r, (device, j) in enumerate(peers):
            copy = remote(buf.at[j, :, cols], dst.at[l, :, cols], d_send.at[c, r], d_recv.at[c, r], device)
            copy.start()
            group.append(copy)
        sent.append(group)
        if c >= 2:

            @pl.when(odd)
            def _(c=c):
                if c == 2:
                    for copy in partly:
                        copy.wait()
                for i in range(2 * (c - 2), 2 * (c - 1)):
                    settle(i)

        own.append(load(buf.at[l, :, cols], dst.at[l, :, cols], own_sem.at[c]))

    for c in range(2):
        own[c].wait()
        for copy in sent[c]:
            copy.wait_recv()
    outs = [load(x, x_out, out_sem.at[0])]

    @pl.when(jnp.logical_not(odd))
    def _():
        for copy in whole:
            copy.wait()

    @pl.when(odd)
    def _():
        for i in range(4, 2 * PIECES):
            settle(i)
        for copy in passes[: 2 * PIECES]:
            copy.wait_recv()

    outs.append(load(wgu, wgu_out, out_sem.at[3]))
    for n in range(ff // TILE):
        gate_at = slice(n * TILE, (n + 1) * TILE)
        up_at = slice(ff + n * TILE, ff + (n + 1) * TILE)
        rows = x[...].reshape(PLANE * ROWS, width)
        gate = jnp.dot(rows, wgu[:, gate_at], preferred_element_type=F32)
        up = jnp.dot(rows, wgu[:, up_at], preferred_element_type=F32)
        pre[:, gate_at] = gate
        pre[:, up_at] = up
        hid[:, gate_at] = (gate * jax.nn.sigmoid(gate) * up).astype(BF16)

        @pl.when(odd)
        def _(n=n):
            settle(2 * PIECES + n)

    outs.append(load(pre, pre_out, out_sem.at[1]))
    outs.append(load(hid, hid_out, out_sem.at[2]))

    @pl.when(odd)
    def _():
        for i in range(2 * PIECES + ff // TILE, 3 * PIECES):
            settle(i)
    whole_down = pltpu.make_async_copy(wdv, wd_out, out_sem.at[4])
    eo_copy = pltpu.make_async_copy(eo, eo_out, out_sem.at[0])

    @pl.when(jnp.logical_not(odd))
    def _():
        whole_down.start()

        def project(n, _):
            at = columns(n)
            eo[:, at] = jnp.dot(hid[...], wdv[:, at], preferred_element_type=F32).astype(BF16)
            return 0

        lax.fori_loop(0, width // TILE, project, 0)
        outs[0].wait()
        eo_copy.start()

    @pl.when(odd)
    def _():
        outs[0].wait()

    for c in range(2, 4):
        own[c].wait()
        for copy in sent[c]:
            copy.wait_recv()
    for copy in outs[1:]:
        copy.wait()

    @pl.when(jnp.logical_not(odd))
    def _():
        eo_copy.wait()
        whole_down.wait()

    @pl.when(odd)
    def _():
        for copy in passes[2 * PIECES :]:
            copy.wait_recv()
        for copy in keeps:
            copy.wait()

    for copy in copies + [g for group in gather + sent for g in group]:
        copy.wait_send()

    @pl.when(odd)
    def _():
        for copy in swaps + passes:
            copy.wait_send()


def dispatch(ids, comb, table, tok, cot, wg, wu, wd):
    width = tok.shape[1]
    ff = wg.shape[1]
    rows = PLANE * ROWS
    vmem = pl.BlockSpec(memory_space=pltpu.VMEM)
    hbm = pl.BlockSpec(memory_space=pl.ANY)
    row_shape = jax.ShapeDtypeStruct((PLANE, ROWS, width), BF16)
    row_buffer = pltpu.VMEM((PLANE, ROWS, width), BF16)
    dma = pltpu.SemaphoreType.DMA
    return pl.pallas_call(
        dispatch_kernel,
        name="dispatch",
        out_shape=(
            row_shape,
            row_shape,
            jax.ShapeDtypeStruct((RINGS, 8, 128), F32),
            jax.ShapeDtypeStruct((rows, 2 * ff), F32),
            jax.ShapeDtypeStruct((rows, ff), BF16),
            jax.ShapeDtypeStruct((width, 2 * ff), BF16),
            jax.ShapeDtypeStruct((ff, width), BF16),
            jax.ShapeDtypeStruct((rows, width), BF16),
        ),
        in_specs=[vmem] * 5 + [hbm] * 3,
        out_specs=(hbm, hbm, vmem, hbm, hbm, hbm, hbm, hbm),
        scratch_shapes=[
            pltpu.VMEM((512, width), BF16),
            pltpu.VMEM((512, width), BF16),
            pltpu.VMEM((rows, 512), BF16),
            pltpu.VMEM((rows, 1), F32),
            row_buffer,
            row_buffer,
            row_buffer,
            pltpu.VMEM((width, 2 * ff), BF16),
            pltpu.VMEM((ff, width), BF16),
            pltpu.VMEM((rows, 2 * ff), F32),
            pltpu.VMEM((rows, ff), BF16),
            pltpu.VMEM((width // 2, 2 * ff), BF16),
            pltpu.VMEM((ff // 2, width), BF16),
            pltpu.VMEM((rows, width), BF16),
            dma((3,)), dma((3,)), dma((4, 3)), dma((4, 3)), dma((4,)), dma((4, 15)), dma((4, 15)),
            dma((3,)), dma((5,)), *[dma((3 * PIECES,)) for _ in range(4)], dma((PIECES,)),
        ],
        compiler_params=pltpu.CompilerParams(
            collective_id=0, has_side_effects=True, vmem_limit_bytes=60 * 2**20
        ),
    )(ids, comb, table, tok, cot, wg, wu, wd)


DOWN = 128
WIDE = 256
NARROW = 128


def finish_kernel(
    x_in, og_in, pre_in, hid_in, meta, table, wgu_in, wd_in, eo_in,
    mixed, input_grad, own_down, own_wide,
    x, og, pre, hid, wgu, wdv, gu, rg, ret, whi, wlo, pick, acc, part, own, gath,
    oth_down, oth_wide, x_down, x_wide, got_down, got_wide,
    in_sem, x_send, x_recv, y_send, y_recv, s_sem, own_sem, p_send, p_recv, b_send, b_recv,
):
    p, l, y = place()
    tokens, width = mixed.shape
    ff = hid.shape[1]
    rows_all = PLANE * ROWS
    ring = [ring_peer(p, l, y, d) for d in range(1, RINGS)]
    peers = [plane_peer(p, l, y, r) for r in range(1, PLANE)]
    across = (1 - p, y * PLANE + l)
    ready = greet(ring + [d for d, _ in peers] + [across])
    loads = [
        load(hid_in, hid, in_sem.at[0]),
        load(og_in, og, in_sem.at[1]),
        load(wd_in, wdv, in_sem.at[2]),
        load(pre_in, pre, in_sem.at[3]),
        load(x_in, x, in_sem.at[4]),
        load(wgu_in, wgu, in_sem.at[5]),
    ]
    even = lax.rem(l, 2) == 0
    eo_copy = pltpu.make_async_copy(eo_in, part.at[pl.ds(0, rows_all)], in_sem.at[6])
    pl.when(even)(eo_copy.start)
    fresh = pre
    downs = (ff // 2) // DOWN
    narrows = (width // 2) // NARROW
    chunks = downs + narrows

    def slab(c, down, wide):
        if c < downs:
            return down.at[pl.ds(c * DOWN, DOWN)]
        return wide.at[pl.ds((c - downs) * NARROW, NARROW)]

    def down_part(side, c):
        at = pl.ds(pl.multiple_of(side * (ff // 2) + c * DOWN, DOWN), DOWN)
        left = hid[:, at].T
        return lambda cols: jnp.dot(
            left, og[:, :, cols].reshape(rows_all, -1), preferred_element_type=F32
        )

    def wide_part(side, c):
        at = pl.ds(pl.multiple_of(side * (width // 2) + c * WIDE, WIDE), WIDE)
        left = x[:, :, at].reshape(rows_all, WIDE).T
        return lambda cols: jnp.dot(left, gu[:, cols], preferred_element_type=F32)

    spans = [pl.ds(0, width), pl.ds(0, width // 2), pl.ds(width // 2, width // 2)]

    def returned(group, j):
        if group == 0:
            return part.at[pl.ds(pl.multiple_of(j * ROWS, ROWS), ROWS)]
        return rg.at[j, :, spans[group]]

    def landing(group):
        return ret.at[0, l] if group == 0 else ret.at[1, l, :, spans[group]]

    back = [[], [], []]
    for group in range(3):
        for r, (device, j) in enumerate(peers):
            back[group].append(
                remote(
                    returned(group, j), landing(group), p_send.at[group, r], p_recv.at[group, r], device
                )
            )
        back[group].append(
            pltpu.make_async_copy(returned(group, l), landing(group), own_sem.at[group])
        )
    x_copies = [
        remote(slab(c, oth_down, oth_wide), slab(c, x_down, x_wide), x_send.at[c], x_recv.at[c], across)
        for c in range(chunks)
    ]
    y_copies = [
        remote(slab(c, x_down, x_wide), slab(c, got_down, got_wide), y_send.at[c], y_recv.at[c], ring[1])
        for c in range(chunks)
    ]
    kept = [
        pltpu.make_async_copy(slab(c, x_down, x_wide), slab(c, own_down, own_wide), s_sem.at[c])
        for c in range(chunks)
    ]

    def project(n, _):
        at = columns(n)
        got = jnp.dot(hid[...], wdv[:, at], preferred_element_type=F32)
        part[0:rows_all, at] = got.astype(BF16)
        return 0

    ready()

    @pl.when(even)
    def _():
        eo_copy.wait()
        for copy in back[0]:
            copy.start()

    loads[0].wait()
    loads[1].wait()
    for c in range(downs):
        part_of = down_part(1 - p, c)
        for n in range(width // 512):
            cols = slice(n * 512, (n + 1) * 512)
            oth_down[c * DOWN : (c + 1) * DOWN, cols] = (0.5 * part_of(cols)).astype(BF16)
        pl.when(even)(x_copies[c].start)
        if c == 0:
            loads[2].wait()

            @pl.when(jnp.logical_not(even))
            def _():
                lax.fori_loop(0, width // TILE, project, 0)
                for copy in back[0]:
                    copy.start()

    loads[3].wait()

    def backward(n, _):
        gate_at = columns(n)
        up_at = columns(ff // TILE + n)
        grad = lax.dot_general(
            og[...].reshape(rows_all, width), wdv[gate_at, :], CONTRACT_LAST, preferred_element_type=F32
        )
        gate, up = pre[:, gate_at], pre[:, up_at]
        sigma = jax.nn.sigmoid(gate)
        gu[:, gate_at] = (grad * up * sigma * (1.0 + gate * (1.0 - sigma))).astype(BF16)
        gu[:, up_at] = (grad * gate * sigma).astype(BF16)
        return 0

    lax.fori_loop(0, ff // TILE, backward, 0)
    loads[4].wait()
    per = WIDE // NARROW
    for c in range(narrows // per):
        part_of = wide_part(1 - p, c)
        for n in range(2):
            cols = slice(n * ff, (n + 1) * ff)
            oth_wide[c * WIDE : (c + 1) * WIDE, cols] = (0.5 * part_of(cols)).astype(BF16)
        for i in range(per):
            pl.when(even)(x_copies[downs + c * per + i].start)
    loads[5].wait()

    def pull(n, _):
        at = columns(n)
        got = lax.dot_general(gu[...], wgu[at, :], CONTRACT_LAST, preferred_element_type=F32)
        rg[:, :, at] = got.astype(BF16).reshape(PLANE, ROWS, TILE)
        return 0

    lax.fori_loop(0, width // TILE, pull, 0)
    for copy in back[1] + back[2]:
        copy.start()
    for b in range(RINGS):
        hit, weight = selection(meta, y * PLANE * ROWS, b)
        at = slice(b * tokens, (b + 1) * tokens)
        weight = weight.T
        high = weight.astype(BF16)
        pick[at, :] = hit.T.astype(BF16)
        whi[at, :] = high
        wlo[at, :] = (weight - high.astype(F32)).astype(BF16)

    own_rows = pl.ds(pl.multiple_of(y * tokens, tokens), tokens)
    summed = [[], []]

    def combine(group):
        which = min(group, 1)
        for copy in back[group][:-1]:
            copy.wait_recv()
        back[group][-1].wait()
        if group == 0:
            for copy in back[0][:-1]:
                copy.wait_send()
        blocks = which * RINGS * tokens

        def step(n, _):
            at = columns(n)
            rows = ret[which, :, :, at].reshape(rows_all, TILE)
            if which == 0:
                total = jnp.dot(whi[...], rows, preferred_element_type=F32)
                total += jnp.dot(wlo[...], rows, preferred_element_type=F32)
            else:
                total = jnp.dot(pick[...], rows, preferred_element_type=F32)
            acc[...] = total
            part[blocks : blocks + RINGS * tokens, at] = total.astype(BF16)
            own[which, :, at] = acc[own_rows, :]
            return 0

        first, size = spans[group].start, spans[group].size
        lax.fori_loop(first // TILE, (first + size) // TILE, step, 0)
        for d in range(3):
            there = pl.ds(pl.multiple_of(blocks + lax.rem(y + d + 1, RINGS) * tokens, tokens), tokens)
            copy = remote(
                part.at[there, spans[group]],
                gath.at[which, d, :, spans[group]],
                b_send.at[group, d],
                b_recv.at[group, d],
                ring[d],
            )
            copy.start()
            summed[which].append(copy)

    def reduce(c):
        if c < downs:
            part_of = down_part(p, c)
            at = slice(c * DOWN, (c + 1) * DOWN)
            x_copies[c].wait_recv()
            for n in range(width // 512):
                cols = slice(n * 512, (n + 1) * 512)
                x_down[at, cols] = (0.5 * part_of(cols) + x_down[at, cols].astype(F32)).astype(BF16)
        else:
            i = c - downs
            if i % per == 0:
                part_of = wide_part(p, i // per)
                for n in range(2):
                    cols = slice(n * ff, (n + 1) * ff)
                    fresh[0:WIDE, cols] = 0.5 * part_of(cols)
            at = slice(i * NARROW, (i + 1) * NARROW)
            x_copies[c].wait_recv()
            mine = fresh[(i % per) * NARROW : (i % per + 1) * NARROW, :]
            x_wide[at, :] = (mine + x_wide[at, :].astype(F32)).astype(BF16)

    @pl.when(even)
    def _():
        for c in range(EARLY):
            reduce(c)
            y_copies[c].start()

    combine(0)

    @pl.when(even)
    def _():
        for c in range(EARLY, chunks):
            reduce(c)
            y_copies[c].start()

    @pl.when(jnp.logical_not(even))
    def _():
        for copy in x_copies:
            copy.start()

    combine(1)
    combine(2)

    @pl.when(even)
    def _():
        take = moving(table, p, l, y)
        for c in range(chunks):
            y_copies[c].wait()
            mine, got = slab(c, x_down, x_wide), slab(c, got_down, got_wide)
            mine[...] = jnp.where(take, got[...].astype(F32), mine[...].astype(F32)).astype(BF16)
            kept[c].start()

    @pl.when(jnp.logical_not(even))
    def _():
        for c in range(chunks):
            reduce(c)
            kept[c].start()

    for which, out in enumerate((mixed, input_grad)):
        total = own[which]
        for copy in summed[which]:
            copy.wait_recv()
        for d in range(3):
            total += gath[which, d].astype(F32)
        out[...] = total.astype(BF16)
    for copy in kept:
        copy.wait()
    for copy in back[1][:-1] + back[2][:-1] + x_copies + summed[0] + summed[1]:
        copy.wait_send()


EARLY = 8


def finish(x, og, pre, hid, meta, table, wgu, wd, eo):
    width = x.shape[-1]
    ff = hid.shape[1]
    rows = PLANE * ROWS
    vmem = pl.BlockSpec(memory_space=pltpu.VMEM)
    hbm = pl.BlockSpec(memory_space=pl.ANY)
    dma = pltpu.SemaphoreType.DMA
    chunks = (ff // 2) // DOWN + (width // 2) // NARROW
    row_shape = jax.ShapeDtypeStruct((128, width), BF16)
    row_buffer = pltpu.VMEM((PLANE, ROWS, width), BF16)
    down_shape, wide_shape = (ff // 2, width), (width // 2, 2 * ff)
    grads = [jax.ShapeDtypeStruct(s, BF16) for s in (down_shape, wide_shape)]
    slabs = [pltpu.VMEM(s, BF16) for s in (down_shape, wide_shape)]
    return pl.pallas_call(
        finish_kernel,
        name="finish",
        out_shape=(row_shape, row_shape, *grads),
        in_specs=[hbm] * 4 + [vmem] * 2 + [hbm] * 3,
        out_specs=(vmem, vmem, hbm, hbm),
        scratch_shapes=[
            row_buffer,
            row_buffer,
            pltpu.VMEM((rows, 2 * ff), F32),
            pltpu.VMEM((rows, ff), BF16),
            pltpu.VMEM((width, 2 * ff), BF16),
            pltpu.VMEM((ff, width), BF16),
            pltpu.VMEM((rows, 2 * ff), BF16),
            row_buffer,
            pltpu.VMEM((2, PLANE, ROWS, width), BF16),
            pltpu.VMEM((512, rows), BF16),
            pltpu.VMEM((512, rows), BF16),
            pltpu.VMEM((512, rows), BF16),
            pltpu.VMEM((512, TILE), F32),
            pltpu.VMEM((2 * 512, width), BF16),
            pltpu.VMEM((2, 128, width), F32),
            pltpu.VMEM((2, 3, 128, width), BF16),
            *slabs,
            *slabs,
            *slabs,
            dma((7,)), dma((chunks,)), dma((chunks,)), dma((chunks,)), dma((chunks,)), dma((chunks,)),
            dma((3,)), dma((3, 15)), dma((3, 15)), dma((3, 3)), dma((3, 3)),
        ],
        compiler_params=pltpu.CompilerParams(
            collective_id=1, has_side_effects=True, vmem_limit_bytes=63 * 2**20
        ),
    )(x, og, pre, hid, meta, table, wgu, wd, eo)


def body(tokens, cotangent, expert_ids, combine, placement, moves, w_gate, w_up, w_down):
    weights = (w_gate[0], w_up[0], w_down[0])
    ff = weights[0].shape[1]
    table = jnp.stack([placement, moves], axis=1)
    x, og, meta, pre, hid, wgu, wd, eo = dispatch(
        expert_ids.T, combine.T, table, tokens, cotangent, *weights
    )
    mixed, input_grad, down, wide = finish(x, og, pre, hid, meta, table, wgu, wd, eo)
    gate, up = wide[:, :ff], wide[:, ff:]
    return (mixed, input_grad) + tuple(g.astype(F32)[None] for g in (gate, up, down))


def solution(mesh):
    tok = P(("dp", "expert"), None)
    weight = P("expert", None, None)
    grad = P("expert", "dp", None)
    return jax.shard_map(
        body,
        mesh=mesh,
        in_specs=(tok, tok, tok, tok, P(), P(), weight, weight, weight),
        out_specs=(tok, tok, grad, grad, grad),
        check_vma=False,
    )
```

```python
import jax
import jax.numpy as jnp
from jax import lax
from jax.experimental import pallas as pl
from jax.experimental.pallas import tpu as pltpu
from jax.sharding import PartitionSpec as P

MESH = pl.DeviceIdType.MESH
BF16 = jnp.bfloat16
F32 = jnp.float32
PLANE = 16
RINGS = 4
CAP = 12
ROWS = RINGS * CAP
TILE = 256
CONTRACT_LAST = (((1,), (1,)), ((), ()))


def place():
    p = lax.axis_index("dp")
    e = lax.axis_index("expert")
    return p, lax.rem(e, PLANE), e // PLANE


def plane_peer(p, l, y, r):
    rc, rx, rz = r % 2, (r // 2) % 2, r // 4
    core, xh, z = lax.rem(l, 2), lax.rem(l // 2, 2), l // 4
    j = lax.rem(z + rz, 4) * 4 + lax.rem(xh + rx, 2) * 2 + lax.rem(core + rc, 2)
    return (p if rx == 0 else 1 - p, y * PLANE + j), j


def plane_source(p, l, y, r):
    rc, rx, rz = r % 2, (r // 2) % 2, r // 4
    core, xh, z = lax.rem(l, 2), lax.rem(l // 2, 2), l // 4
    j = lax.rem(z + 4 - rz, 4) * 4 + lax.rem(xh + rx, 2) * 2 + lax.rem(core + rc, 2)
    return (p if rx == 0 else 1 - p, y * PLANE + j), j


def ring_peer(p, l, y, d):
    return (p, lax.rem(y + d, RINGS) * PLANE + l)


def remote(src, dst, send, recv, device):
    return pltpu.make_async_remote_copy(
        src_ref=src, dst_ref=dst, send_sem=send, recv_sem=recv, device_id=device, device_id_type=MESH
    )


def greet(devices):
    barrier = pltpu.get_barrier_semaphore()
    for device in devices:
        pl.semaphore_signal(barrier, inc=1, device_id=device, device_id_type=MESH)
    return lambda: pl.semaphore_wait(barrier, len(devices))


def columns(n):
    return pl.ds(pl.multiple_of(n * TILE, TILE), TILE)


def selection(meta, base, ring):
    m = meta[ring]
    row = (lax.broadcasted_iota(jnp.int32, (PLANE * ROWS, 128), 0) + base).astype(F32)
    hit = jnp.zeros((PLANE * ROWS, 128), F32)
    weight = jnp.zeros((PLANE * ROWS, 128), F32)
    for k in range(4):
        same = row == m[k : k + 1, :]
        hit = jnp.where(same, 1.0, hit)
        weight = jnp.where(same, m[4 + k : 5 + k, :], weight)
    return hit, weight


def moving(table, p, l, y):
    slot = lax.broadcasted_iota(jnp.int32, (table.shape[0], 1), 0)
    mine = jnp.where(slot == y * PLANE + l, table[:, 1:2], 0)
    return jnp.sum(mine.astype(F32), axis=0, keepdims=True) > 0.0


def load(src, dst, sem):
    copy = pltpu.make_async_copy(src, dst, sem)
    copy.start()
    return copy


PIECES = 4


def dispatch_kernel(
    ids, comb, table, tok, cot, wg, wu, wd,
    x_out, og_out, meta, pre_out, hid_out, wgu_out, wd_out, eo_out,
    gtok, gcot, pick, rw, sx, so, x, wgu, wdv, pre, hid, new_wide, new_down, eo,
    meta_send, meta_recv, ag_send, ag_recv, own_sem, d_send, d_recv, w_sem, out_sem,
    swap_send, swap_recv, pass_send, pass_recv, keep_sem,
):
    p, l, y = place()
    width = tok.shape[1]
    ff = wg.shape[1]
    half = width // 2
    ring = [ring_peer(p, l, y, d) for d in range(1, RINGS)]
    peers = [plane_peer(p, l, y, r) for r in range(1, PLANE)]
    across = (1 - p, y * PLANE + l)
    ready = greet(ring + [d for d, _ in peers] + [across])
    odd = lax.rem(l, 2) == 1
    wide_half, down_half = width // 2, ff // 2
    wide_rows = pl.ds(pl.multiple_of(p * wide_half, wide_half), wide_half)
    down_rows = pl.ds(pl.multiple_of(p * down_half, down_half), down_half)
    whole = [
        pltpu.make_async_copy(wg, wgu.at[:, pl.ds(0, ff)], w_sem.at[0]),
        pltpu.make_async_copy(wu, wgu.at[:, pl.ds(ff, ff)], w_sem.at[1]),
        pltpu.make_async_copy(wd, wdv, w_sem.at[2]),
    ]
    partly = [
        pltpu.make_async_copy(wg.at[wide_rows], wgu.at[wide_rows, pl.ds(0, ff)], w_sem.at[0]),
        pltpu.make_async_copy(wu.at[wide_rows], wgu.at[wide_rows, pl.ds(ff, ff)], w_sem.at[1]),
        pltpu.make_async_copy(wd.at[down_rows], wdv.at[down_rows], w_sem.at[2]),
    ]
    swaps, passes, pieces, keeps = [], [], [], []
    for i in range(3 * PIECES):
        which, piece = i // PIECES, i % PIECES
        size = (wide_half if which < 2 else down_half) // PIECES
        source = (wg, wu, wd)[which]
        at = pl.ds(pl.multiple_of(p * PIECES * size + piece * size, size), size)
        near = pl.ds(piece * size, size)
        if which < 2:
            landed = new_wide.at[near, pl.ds(which * ff, ff)]
            held = wgu.at[at, pl.ds(which * ff, ff)]
        else:
            landed = new_down.at[near]
            held = wdv.at[at]
        swaps.append(remote(source.at[at], landed, swap_send.at[i], swap_recv.at[i], ring[1]))
        final = held if which < 2 else wd_out.at[at]
        passes.append(remote(held, final, pass_send.at[i], pass_recv.at[i], across))
        if which == 2:
            keeps.append(pltpu.make_async_copy(held, final, keep_sem.at[piece]))
        pieces.append((landed, held))

    take = moving(table, p, l, y)

    def settle(i):
        landed, held = pieces[i]
        swaps[i].wait_recv()
        held[...] = jnp.where(take, landed[...].astype(F32), held[...].astype(F32)).astype(BF16)
        passes[i].start()
        if i >= 2 * PIECES:
            keeps[i - 2 * PIECES].start()

    @pl.when(odd)
    def _():
        for copy in partly:
            copy.start()

    @pl.when(jnp.logical_not(odd))
    def _():
        for copy in whole:
            copy.start()

    slots = table.shape[0]
    tokens = ids.shape[1]
    slot_id = lax.broadcasted_iota(jnp.int32, (slots, tokens), 0)
    plc, moves = table[:, 0:1], table[:, 1:2]
    paired = jnp.concatenate([plc[slots // 2 :], plc[: slots // 2]], axis=0)
    one = lax.broadcasted_iota(jnp.int32, (slots, 1), 0)
    located = jnp.where((lax.rem(one, 2) == 1) & (moves == 1), paired, plc)
    owned = [(located == ids[k : k + 1, :]) for k in range(4)]
    member = jnp.zeros((slots, tokens), F32)
    for o in owned:
        member = jnp.where(o, 1.0, member)
    before = (
        lax.broadcasted_iota(jnp.int32, (tokens, tokens), 0)
        < lax.broadcasted_iota(jnp.int32, (tokens, tokens), 1)
    ).astype(F32)
    rank = jnp.dot(member.astype(BF16), before.astype(BF16), preferred_element_type=F32)
    position = rank + (slot_id * ROWS + y * CAP).astype(F32)
    rows = [jnp.sum(jnp.where(o, position, 0.0), axis=0, keepdims=True) for o in owned]
    meta[y] = jnp.concatenate(rows + [comb[...]], axis=0)
    own_rows = pl.ds(pl.multiple_of(y * tokens, tokens), tokens)

    ready()
    copies = [
        remote(meta.at[y], meta.at[y], meta_send.at[d], meta_recv.at[d], ring[d]) for d in range(3)
    ]
    gather = []
    for c in range(4):
        src, dst = (tok, gtok) if c < 2 else (cot, gcot)
        cols = pl.ds((c % 2) * half, half)
        gather.append([
            remote(src.at[:, cols], dst.at[own_rows, cols], ag_send.at[c, d], ag_recv.at[c, d], ring[d])
            for d in range(3)
        ])
    for copy in copies + [g for group in gather for g in group]:
        copy.start()
    gtok[own_rows, :] = tok[...]
    gcot[own_rows, :] = cot[...]
    for copy in copies:
        copy.wait_recv()
    for b in range(RINGS):
        hit, weight = selection(meta, y * PLANE * ROWS, b)
        pick[:, b * tokens : (b + 1) * tokens] = hit.astype(BF16)
        total = jnp.sum(weight, axis=1, keepdims=True)
        rw[...] = total if b == 0 else rw[...] + total

    sent, own = [], []
    for c in range(4):
        src, buf, dst = (gtok, sx, x) if c < 2 else (gcot, so, og_out)
        cols = pl.ds((c % 2) * half, half)
        for copy in gather[c]:
            copy.wait_recv()
        if c == 1:

            @pl.when(odd)
            def _():
                for copy in swaps:
                    copy.start()

        def step(n, _, src=src, buf=buf, c=c):
            at = columns((c % 2) * (half // TILE) + n)
            got = jnp.dot(pick[...], src[:, at], preferred_element_type=F32)
            if c >= 2:
                got = rw[...] * got
            buf[:, :, at] = got.astype(BF16).reshape(PLANE, ROWS, TILE)
            return 0

        lax.fori_loop(0, half // TILE, step, 0)
        group = []
        for r, (device, j) in enumerate(peers):
            copy = remote(buf.at[j, :, cols], dst.at[l, :, cols], d_send.at[c, r], d_recv.at[c, r], device)
            copy.start()
            group.append(copy)
        sent.append(group)
        if c >= 2:

            @pl.when(odd)
            def _(c=c):
                if c == 2:
                    for copy in partly:
                        copy.wait()
                for i in range(2 * (c - 2), 2 * (c - 1)):
                    settle(i)

        own.append(load(buf.at[l, :, cols], dst.at[l, :, cols], own_sem.at[c]))

    for c in range(2):
        own[c].wait()
        for copy in sent[c]:
            copy.wait_recv()
    outs = [load(x, x_out, out_sem.at[0])]

    @pl.when(jnp.logical_not(odd))
    def _():
        for copy in whole:
            copy.wait()

    @pl.when(odd)
    def _():
        for i in range(4, 2 * PIECES):
            settle(i)
        for copy in passes[: 2 * PIECES]:
            copy.wait_recv()

    outs.append(load(wgu, wgu_out, out_sem.at[3]))
    for n in range(ff // TILE):
        gate_at = slice(n * TILE, (n + 1) * TILE)
        up_at = slice(ff + n * TILE, ff + (n + 1) * TILE)
        rows = x[...].reshape(PLANE * ROWS, width)
        gate = jnp.dot(rows, wgu[:, gate_at], preferred_element_type=F32)
        up = jnp.dot(rows, wgu[:, up_at], preferred_element_type=F32)
        pre[:, gate_at] = gate
        pre[:, up_at] = up
        hid[:, gate_at] = (gate * jax.nn.sigmoid(gate) * up).astype(BF16)

        @pl.when(odd)
        def _(n=n):
            settle(2 * PIECES + n)

    outs.append(load(pre, pre_out, out_sem.at[1]))
    outs.append(load(hid, hid_out, out_sem.at[2]))

    @pl.when(odd)
    def _():
        for i in range(2 * PIECES + ff // TILE, 3 * PIECES):
            settle(i)
    whole_down = pltpu.make_async_copy(wdv, wd_out, out_sem.at[4])
    eo_copy = pltpu.make_async_copy(eo, eo_out, out_sem.at[0])

    @pl.when(jnp.logical_not(odd))
    def _():
        whole_down.start()

        def project(n, _):
            at = columns(n)
            eo[:, at] = jnp.dot(hid[...], wdv[:, at], preferred_element_type=F32).astype(BF16)
            return 0

        lax.fori_loop(0, width // TILE, project, 0)
        outs[0].wait()
        eo_copy.start()

    @pl.when(odd)
    def _():
        outs[0].wait()

    for c in range(2, 4):
        own[c].wait()
        for copy in sent[c]:
            copy.wait_recv()
    for copy in outs[1:]:
        copy.wait()

    @pl.when(jnp.logical_not(odd))
    def _():
        eo_copy.wait()
        whole_down.wait()

    @pl.when(odd)
    def _():
        for copy in passes[2 * PIECES :]:
            copy.wait_recv()
        for copy in keeps:
            copy.wait()

    for copy in copies + [g for group in gather + sent for g in group]:
        copy.wait_send()

    @pl.when(odd)
    def _():
        for copy in swaps + passes:
            copy.wait_send()


def dispatch(ids, comb, table, tok, cot, wg, wu, wd):
    width = tok.shape[1]
    ff = wg.shape[1]
    rows = PLANE * ROWS
    vmem = pl.BlockSpec(memory_space=pltpu.VMEM)
    hbm = pl.BlockSpec(memory_space=pl.ANY)
    row_shape = jax.ShapeDtypeStruct((PLANE, ROWS, width), BF16)
    row_buffer = pltpu.VMEM((PLANE, ROWS, width), BF16)
    dma = pltpu.SemaphoreType.DMA
    return pl.pallas_call(
        dispatch_kernel,
        name="dispatch",
        out_shape=(
            row_shape,
            row_shape,
            jax.ShapeDtypeStruct((RINGS, 8, 128), F32),
            jax.ShapeDtypeStruct((rows, 2 * ff), F32),
            jax.ShapeDtypeStruct((rows, ff), BF16),
            jax.ShapeDtypeStruct((width, 2 * ff), BF16),
            jax.ShapeDtypeStruct((ff, width), BF16),
            jax.ShapeDtypeStruct((rows, width), BF16),
        ),
        in_specs=[vmem] * 5 + [hbm] * 3,
        out_specs=(hbm, hbm, vmem, hbm, hbm, hbm, hbm, hbm),
        scratch_shapes=[
            pltpu.VMEM((512, width), BF16),
            pltpu.VMEM((512, width), BF16),
            pltpu.VMEM((rows, 512), BF16),
            pltpu.VMEM((rows, 1), F32),
            row_buffer,
            row_buffer,
            row_buffer,
            pltpu.VMEM((width, 2 * ff), BF16),
            pltpu.VMEM((ff, width), BF16),
            pltpu.VMEM((rows, 2 * ff), F32),
            pltpu.VMEM((rows, ff), BF16),
            pltpu.VMEM((width // 2, 2 * ff), BF16),
            pltpu.VMEM((ff // 2, width), BF16),
            pltpu.VMEM((rows, width), BF16),
            dma((3,)), dma((3,)), dma((4, 3)), dma((4, 3)), dma((4,)), dma((4, 15)), dma((4, 15)),
            dma((3,)), dma((5,)), *[dma((3 * PIECES,)) for _ in range(4)], dma((PIECES,)),
        ],
        compiler_params=pltpu.CompilerParams(
            collective_id=0, has_side_effects=True, vmem_limit_bytes=60 * 2**20
        ),
    )(ids, comb, table, tok, cot, wg, wu, wd)


DOWN = 128
WIDE = 256
NARROW = 128


def finish_kernel(
    x_in, og_in, pre_in, hid_in, meta, table, wgu_in, wd_in, eo_in,
    mixed, input_grad, own_down, own_wide,
    x, og, pre, hid, wgu, wdv, gu, rg, ret, whi, wlo, pick, acc, part, own, gath,
    oth_down, oth_wide, x_down, x_wide, got_down, got_wide,
    in_sem, x_send, x_recv, y_send, y_recv, s_sem, own_sem, p_send, p_recv, b_send, b_recv,
):
    p, l, y = place()
    tokens, width = mixed.shape
    ff = hid.shape[1]
    rows_all = PLANE * ROWS
    ring = [ring_peer(p, l, y, d) for d in range(1, RINGS)]
    peers = [plane_peer(p, l, y, r) for r in range(1, PLANE)]
    across = (1 - p, y * PLANE + l)
    ready = greet(ring + [d for d, _ in peers] + [across])
    loads = [
        load(hid_in, hid, in_sem.at[0]),
        load(og_in, og, in_sem.at[1]),
        load(wd_in, wdv, in_sem.at[2]),
        load(pre_in, pre, in_sem.at[3]),
        load(x_in, x, in_sem.at[4]),
        load(wgu_in, wgu, in_sem.at[5]),
    ]
    even = lax.rem(l, 2) == 0
    eo_copy = pltpu.make_async_copy(eo_in, part.at[pl.ds(0, rows_all)], in_sem.at[6])
    pl.when(even)(eo_copy.start)
    fresh = pre
    downs = (ff // 2) // DOWN
    narrows = (width // 2) // NARROW
    chunks = downs + narrows

    def slab(c, down, wide):
        if c < downs:
            return down.at[pl.ds(c * DOWN, DOWN)]
        return wide.at[pl.ds((c - downs) * NARROW, NARROW)]

    def down_part(side, c):
        at = pl.ds(pl.multiple_of(side * (ff // 2) + c * DOWN, DOWN), DOWN)
        left = hid[:, at].T
        return lambda cols: jnp.dot(
            left, og[:, :, cols].reshape(rows_all, -1), preferred_element_type=F32
        )

    def wide_part(side, c):
        at = pl.ds(pl.multiple_of(side * (width // 2) + c * WIDE, WIDE), WIDE)
        left = x[:, :, at].reshape(rows_all, WIDE).T
        return lambda cols: jnp.dot(left, gu[:, cols], preferred_element_type=F32)

    spans = [pl.ds(0, width)] + [pl.ds(i * (width // 4), width // 4) for i in range(4)]

    def returned(group, j):
        if group == 0:
            return part.at[pl.ds(pl.multiple_of(j * ROWS, ROWS), ROWS)]
        return rg.at[j, :, spans[group]]

    def landing(group):
        return ret.at[0, l] if group == 0 else ret.at[1, l, :, spans[group]]

    back = [[] for _ in spans]
    for group in range(len(spans)):
        for r, (device, j) in enumerate(peers):
            back[group].append(
                remote(
                    returned(group, j), landing(group), p_send.at[group, r], p_recv.at[group, r], device
                )
            )
        back[group].append(
            pltpu.make_async_copy(returned(group, l), landing(group), own_sem.at[group])
        )
    x_copies = [
        remote(slab(c, oth_down, oth_wide), slab(c, x_down, x_wide), x_send.at[c], x_recv.at[c], across)
        for c in range(chunks)
    ]
    y_copies = [
        remote(slab(c, x_down, x_wide), slab(c, got_down, got_wide), y_send.at[c], y_recv.at[c], ring[1])
        for c in range(chunks)
    ]
    kept = [
        pltpu.make_async_copy(slab(c, x_down, x_wide), slab(c, own_down, own_wide), s_sem.at[c])
        for c in range(chunks)
    ]

    def project(n, _):
        at = columns(n)
        got = jnp.dot(hid[...], wdv[:, at], preferred_element_type=F32)
        part[0:rows_all, at] = got.astype(BF16)
        return 0

    ready()

    @pl.when(even)
    def _():
        eo_copy.wait()
        for copy in back[0]:
            copy.start()

    loads[0].wait()
    loads[1].wait()
    for c in range(downs):
        part_of = down_part(1 - p, c)
        for n in range(width // 512):
            cols = slice(n * 512, (n + 1) * 512)
            oth_down[c * DOWN : (c + 1) * DOWN, cols] = (0.5 * part_of(cols)).astype(BF16)
        pl.when(even)(x_copies[c].start)
        if c == 0:
            loads[2].wait()

            @pl.when(jnp.logical_not(even))
            def _():
                lax.fori_loop(0, width // TILE, project, 0)
                for copy in back[0]:
                    copy.start()

    loads[3].wait()

    def backward(n, _):
        gate_at = columns(n)
        up_at = columns(ff // TILE + n)
        grad = lax.dot_general(
            og[...].reshape(rows_all, width), wdv[gate_at, :], CONTRACT_LAST, preferred_element_type=F32
        )
        gate, up = pre[:, gate_at], pre[:, up_at]
        sigma = jax.nn.sigmoid(gate)
        gu[:, gate_at] = (grad * up * sigma * (1.0 + gate * (1.0 - sigma))).astype(BF16)
        gu[:, up_at] = (grad * gate * sigma).astype(BF16)
        return 0

    lax.fori_loop(0, ff // TILE, backward, 0)
    loads[4].wait()
    per = WIDE // NARROW
    for c in range(narrows // per):
        part_of = wide_part(1 - p, c)
        for n in range(2):
            cols = slice(n * ff, (n + 1) * ff)
            oth_wide[c * WIDE : (c + 1) * WIDE, cols] = (0.5 * part_of(cols)).astype(BF16)
        for i in range(per):
            pl.when(even)(x_copies[downs + c * per + i].start)
    loads[5].wait()

    def pull(n, _):
        at = columns(n)
        got = lax.dot_general(gu[...], wgu[at, :], CONTRACT_LAST, preferred_element_type=F32)
        rg[:, :, at] = got.astype(BF16).reshape(PLANE, ROWS, TILE)
        return 0

    lax.fori_loop(0, width // TILE, pull, 0)
    for copy in [b for group in back[1:] for b in group]:
        copy.start()
    for b in range(RINGS):
        hit, weight = selection(meta, y * PLANE * ROWS, b)
        at = slice(b * tokens, (b + 1) * tokens)
        weight = weight.T
        high = weight.astype(BF16)
        pick[at, :] = hit.T.astype(BF16)
        whi[at, :] = high
        wlo[at, :] = (weight - high.astype(F32)).astype(BF16)

    own_rows = pl.ds(pl.multiple_of(y * tokens, tokens), tokens)
    summed = [[], []]

    def combine(group):
        which = min(group, 1)
        for copy in back[group][:-1]:
            copy.wait_recv()
        back[group][-1].wait()
        if group == 0:
            for copy in back[0][:-1]:
                copy.wait_send()
        blocks = which * RINGS * tokens

        def step(n, _):
            at = columns(n)
            rows = ret[which, :, :, at].reshape(rows_all, TILE)
            if which == 0:
                total = jnp.dot(whi[...], rows, preferred_element_type=F32)
                total += jnp.dot(wlo[...], rows, preferred_element_type=F32)
            else:
                total = jnp.dot(pick[...], rows, preferred_element_type=F32)
            acc[...] = total
            part[blocks : blocks + RINGS * tokens, at] = total.astype(BF16)
            own[which, :, at] = acc[own_rows, :]
            return 0

        first, size = spans[group].start, spans[group].size
        lax.fori_loop(first // TILE, (first + size) // TILE, step, 0)
        for d in range(3):
            there = pl.ds(pl.multiple_of(blocks + lax.rem(y + d + 1, RINGS) * tokens, tokens), tokens)
            copy = remote(
                part.at[there, spans[group]],
                gath.at[which, d, :, spans[group]],
                b_send.at[group, d],
                b_recv.at[group, d],
                ring[d],
            )
            copy.start()
            summed[which].append(copy)

    def reduce(c):
        if c < downs:
            part_of = down_part(p, c)
            at = slice(c * DOWN, (c + 1) * DOWN)
            x_copies[c].wait_recv()
            for n in range(width // 512):
                cols = slice(n * 512, (n + 1) * 512)
                x_down[at, cols] = (0.5 * part_of(cols) + x_down[at, cols].astype(F32)).astype(BF16)
        else:
            i = c - downs
            if i % per == 0:
                part_of = wide_part(p, i // per)
                for n in range(2):
                    cols = slice(n * ff, (n + 1) * ff)
                    fresh[0:WIDE, cols] = 0.5 * part_of(cols)
            at = slice(i * NARROW, (i + 1) * NARROW)
            x_copies[c].wait_recv()
            mine = fresh[(i % per) * NARROW : (i % per + 1) * NARROW, :]
            x_wide[at, :] = (mine + x_wide[at, :].astype(F32)).astype(BF16)

    @pl.when(even)
    def _():
        for c in range(EARLY):
            reduce(c)
            y_copies[c].start()

    combine(0)

    @pl.when(even)
    def _():
        for c in range(EARLY, chunks):
            reduce(c)
            y_copies[c].start()

    @pl.when(jnp.logical_not(even))
    def _():
        for copy in x_copies:
            copy.start()

    for group in range(1, len(spans)):
        combine(group)

    @pl.when(even)
    def _():
        take = moving(table, p, l, y)
        for c in range(chunks):
            y_copies[c].wait()
            mine, got = slab(c, x_down, x_wide), slab(c, got_down, got_wide)
            mine[...] = jnp.where(take, got[...].astype(F32), mine[...].astype(F32)).astype(BF16)
            kept[c].start()

    @pl.when(jnp.logical_not(even))
    def _():
        for c in range(chunks):
            reduce(c)
            kept[c].start()

    for which, out in enumerate((mixed, input_grad)):
        total = own[which]
        for copy in summed[which]:
            copy.wait_recv()
        for d in range(3):
            total += gath[which, d].astype(F32)
        out[...] = total.astype(BF16)
    for copy in kept:
        copy.wait()
    for copy in [b for group in back[1:] for b in group[:-1]] + x_copies + summed[0] + summed[1]:
        copy.wait_send()


EARLY = 8


def finish(x, og, pre, hid, meta, table, wgu, wd, eo):
    width = x.shape[-1]
    ff = hid.shape[1]
    rows = PLANE * ROWS
    vmem = pl.BlockSpec(memory_space=pltpu.VMEM)
    hbm = pl.BlockSpec(memory_space=pl.ANY)
    dma = pltpu.SemaphoreType.DMA
    chunks = (ff // 2) // DOWN + (width // 2) // NARROW
    row_shape = jax.ShapeDtypeStruct((128, width), BF16)
    row_buffer = pltpu.VMEM((PLANE, ROWS, width), BF16)
    down_shape, wide_shape = (ff // 2, width), (width // 2, 2 * ff)
    grads = [jax.ShapeDtypeStruct(s, BF16) for s in (down_shape, wide_shape)]
    slabs = [pltpu.VMEM(s, BF16) for s in (down_shape, wide_shape)]
    return pl.pallas_call(
        finish_kernel,
        name="finish",
        out_shape=(row_shape, row_shape, *grads),
        in_specs=[hbm] * 4 + [vmem] * 2 + [hbm] * 3,
        out_specs=(vmem, vmem, hbm, hbm),
        scratch_shapes=[
            row_buffer,
            row_buffer,
            pltpu.VMEM((rows, 2 * ff), F32),
            pltpu.VMEM((rows, ff), BF16),
            pltpu.VMEM((width, 2 * ff), BF16),
            pltpu.VMEM((ff, width), BF16),
            pltpu.VMEM((rows, 2 * ff), BF16),
            row_buffer,
            pltpu.VMEM((2, PLANE, ROWS, width), BF16),
            pltpu.VMEM((512, rows), BF16),
            pltpu.VMEM((512, rows), BF16),
            pltpu.VMEM((512, rows), BF16),
            pltpu.VMEM((512, TILE), F32),
            pltpu.VMEM((2 * 512, width), BF16),
            pltpu.VMEM((2, 128, width), F32),
            pltpu.VMEM((2, 3, 128, width), BF16),
            *slabs,
            *slabs,
            *slabs,
            dma((7,)), dma((chunks,)), dma((chunks,)), dma((chunks,)), dma((chunks,)), dma((chunks,)),
            dma((5,)), dma((5, 15)), dma((5, 15)), dma((5, 3)), dma((5, 3)),
        ],
        compiler_params=pltpu.CompilerParams(
            collective_id=1, has_side_effects=True, vmem_limit_bytes=63 * 2**20
        ),
    )(x, og, pre, hid, meta, table, wgu, wd, eo)


def body(tokens, cotangent, expert_ids, combine, placement, moves, w_gate, w_up, w_down):
    weights = (w_gate[0], w_up[0], w_down[0])
    ff = weights[0].shape[1]
    table = jnp.stack([placement, moves], axis=1)
    x, og, meta, pre, hid, wgu, wd, eo = dispatch(
        expert_ids.T, combine.T, table, tokens, cotangent, *weights
    )
    mixed, input_grad, down, wide = finish(x, og, pre, hid, meta, table, wgu, wd, eo)
    gate, up = wide[:, :ff], wide[:, ff:]
    return (mixed, input_grad) + tuple(g.astype(F32)[None] for g in (gate, up, down))


def solution(mesh):
    tok = P(("dp", "expert"), None)
    weight = P("expert", None, None)
    grad = P("expert", "dp", None)
    return jax.shard_map(
        body,
        mesh=mesh,
        in_specs=(tok, tok, tok, tok, P(), P(), weight, weight, weight),
        out_specs=(tok, tok, grad, grad, grad),
        check_vma=False,
    )
```
